32 devices in a mesh: feat: 4 (over y, x), tok: 8 (over z, core).
Axes of the slice: x: 2, y: 2, z: 4, core: 2. Of those that a mesh axis runs over, the one named last changes fastest.
Arguments:
- tokens: bfloat16 [2048, 12288], P('tok', 'feat'), may hold values from -6 to 6
- gate_weight: bfloat16 [16, 5, 768, 768], P('feat', None, 'tok'), may hold values from -0.09375 to 0.09375
- up_weight: bfloat16 [16, 5, 768, 768], P('feat', None, 'tok'), may hold values from -0.09375 to 0.09375
- gate_scale: float32 [16, 5], P('feat'), may hold values from 0.35 to 2.8
- up_scale: float32 [16, 5], P('feat'), may hold values from 0.35 to 2.8
- partners: int32 [16, 5], replicated, may hold values from 0 to 15, as said below
- latent_in: bfloat16 [12288, 768], P('feat'), may hold values from -0.0546875 to 0.0546875
- latent_out: bfloat16 [768, 12288], P(None, 'feat'), may hold values from -0.21875 to 0.21875
Outputs:
- hidden: bfloat16 [2048, 12288], P('tok', 'feat')
- rank_term: bfloat16 [2048, 12288], P('tok', 'feat')
The draws below stay inside these ranges and needn't reach their ends.
Inputs may be any that keep to these rules, and one draw needn't show every extreme that they name: `partners`: row i lists the blocks i, i xor 1, i xor 2, i xor 4 and i xor 8, each once, in some order.
All inputs are finite; a program needn't handle non-finite values.
Results may differ from the reference program's by a relative error of at most 0.015.
Values may be sent and summed in bfloat16 or wider, within the bound.
A program may use at most 128 MiB of HBM per device.

```python
import math
import jax
import jax.numpy as jnp
from jax import lax

BLK = 768
NBLK = 16
PART = 5
RANK = 768
D = 12288
TOKENS = 2048


def draw_partners(key, part):
    row_ids = jnp.arange(NBLK, dtype=jnp.int32)
    offsets = jnp.concatenate([jnp.zeros((1,), jnp.int32), jnp.left_shift(jnp.ones((PART - 1,), jnp.int32), jnp.arange(PART - 1, dtype=jnp.int32))])
    base_ids = jnp.bitwise_xor(row_ids[:, None], offsets[None, :])
    row_keys = jax.random.split(jax.random.fold_in(key, 7), NBLK)
    orders = jax.vmap(lambda row_key: jax.random.permutation(row_key, PART))(row_keys)
    return jnp.take_along_axis(base_ids, orders.astype(jnp.int32), axis=1)


def block_scale(own_key, dims, cuts, least, high):
    factor_of, own = 1.0, jax.random.fold_in(own_key, 6)
    for position, parts in cuts:
        draws = jnp.exp(jax.random.uniform(jax.random.fold_in(own, position), (parts,), jnp.float32, least / len(cuts), high / len(cuts)))
        factor_of = factor_of * jnp.repeat(draws, dims[position] // parts).reshape([-1 if axis == position else 1 for axis in range(len(dims))])
    return factor_of


def centred(rng, shape, deviation, limit, cuts=(), kind=jnp.bfloat16):
    drawn = deviation * jax.random.normal(rng, shape, jnp.float32)
    if cuts:
        drawn = drawn * block_scale(rng, shape, cuts, -0.22, 0.18)
    return jnp.clip(drawn, -limit, limit).astype(kind)


def setup_inputs(seed: int = 0) -> dict:
    key_of = jax.random.split(jax.random.key(seed), 9)
    tokens = centred(key_of[0], (TOKENS, D), 1.0, 6.0, ((0, 8), (1, 4)))
    gate_weight = centred(key_of[1], (NBLK, PART, BLK, BLK), (PART * BLK) ** -0.5, 0.09375, ((0, 4), (2, 8)))
    up_weight = centred(key_of[2], (NBLK, PART, BLK, BLK), (PART * BLK) ** -0.5, 0.09375, ((0, 4), (2, 8)))
    gate_scale = jnp.clip(jnp.exp(math.log(2.8) - 2.0794415 * jax.random.uniform(key_of[3], (NBLK, PART), jnp.float32) ** block_scale(key_of[3], (NBLK, PART), ((0, 4),), -0.2, 0.2)), 0.35, 2.8)
    up_scale = jnp.clip(jnp.exp(math.log(2.8) - 2.0794415 * jax.random.uniform(key_of[4], (NBLK, PART), jnp.float32) ** block_scale(key_of[4], (NBLK, PART), ((0, 4),), -0.2, 0.2)), 0.35, 2.8)
    partners = draw_partners(jax.random.fold_in(key_of[8], 71), 0)
    latent_in = centred(key_of[6], (D, RANK), D ** -0.5, 0.0546875, ((0, 4),))
    latent_out = centred(key_of[7], (RANK, D), RANK ** -0.5, 0.21875, ((1, 4),))
    return dict(tokens=tokens, gate_weight=gate_weight, up_weight=up_weight, gate_scale=gate_scale, up_scale=up_scale, partners=partners, latent_in=latent_in, latent_out=latent_out)


def slot_inputs(tokens, row_ids):
    return jnp.stack([lax.dynamic_slice_in_dim(tokens, (row_ids[slot_idx] * BLK).astype(jnp.int32), BLK, 1) for slot_idx in range(PART)])


def reference(tokens, gate_weight, up_weight, gate_scale, up_scale, partners, latent_in, latent_out):
    def one_block(block_id):
        row_ids = partners[block_id]
        inputs = slot_inputs(tokens, row_ids).astype(jnp.float32)
        gate_terms = jnp.einsum("ktb,kbc->ktc", inputs, gate_weight[block_id].astype(jnp.float32))
        up_terms = jnp.einsum("ktb,kbc->ktc", inputs, up_weight[block_id].astype(jnp.float32))
        gate_sum = jnp.sum(gate_terms * gate_scale[block_id][:, None, None], axis=0)
        up_sum = jnp.sum(up_terms * up_scale[block_id][:, None, None], axis=0)
        return (jax.nn.silu(gate_sum) * up_sum).astype(jnp.bfloat16)

    blocks = lax.map(one_block, jnp.arange(NBLK, dtype=jnp.int32))
    hidden = jnp.transpose(blocks, (1, 0, 2)).reshape(TOKENS, NBLK * BLK)
    latent = jnp.dot(hidden, latent_in, preferred_element_type=jnp.float32).astype(jnp.bfloat16)
    rank_term = jnp.dot(latent, latent_out, preferred_element_type=jnp.float32).astype(jnp.bfloat16)
    return hidden, rank_term
```

```python
import functools
import math

import jax
import jax.numpy as jnp
from jax import lax
from jax.experimental import pallas as pl
from jax.experimental.pallas import tpu as pltpu
from jax.sharding import PartitionSpec as P


PAIR = 2


def swapped(value, axis, bit):
    mask = 2**bit
    pairs = [(source, source ^ mask) for source in range(lax.axis_size(axis))]
    return lax.ppermute(value, axis, pairs)


def moved(value, chip_pairs):
    pairs = [
        (PAIR * source + lane, PAIR * target + lane)
        for source, target in chip_pairs
        for lane in range(PAIR)
    ]
    return lax.ppermute(value, "tok", pairs)


def join_kernel(slots, gate, up, gate_scale, up_scale, joined, *, block):
    slot = slots[block, pl.program_id(0)]
    width = gate.shape[-1]
    for start, weight, scale in ((0, gate, gate_scale), (width, up, up_scale)):
        product = weight[0, 0].astype(jnp.float32) * scale[block, slot]
        joined[0, :, start : start + width] = product.astype(joined.dtype)


def joined_weights(slots, gate_weight, up_weight, gate_scale, up_scale, block):
    _, slot_count, rows, width = gate_weight.shape
    picked = pl.BlockSpec((1, 1, rows, width), lambda k, slots: (block, slots[block, k], 0, 0))
    whole = pl.BlockSpec(memory_space=pltpu.SMEM)
    size = slot_count * rows * width
    return pl.pallas_call(
        lambda *refs: join_kernel(*refs, block=block),
        out_shape=jax.ShapeDtypeStruct((slot_count, rows, 2 * width), jnp.bfloat16),
        grid_spec=pltpu.PrefetchScalarGridSpec(
            num_scalar_prefetch=1,
            grid=(slot_count,),
            in_specs=[picked, picked, whole, whole],
            out_specs=pl.BlockSpec((1, rows, 2 * width), lambda k, slots: (k, 0, 0)),
        ),
        cost_estimate=pl.CostEstimate(flops=2 * size, bytes_accessed=8 * size, transcendentals=0),
    )(slots, gate_weight, up_weight, gate_scale, up_scale)


def part_blocks(blocks):
    return max(1, blocks // 2)


def per_device(
    tokens, gate_weight, up_weight, gate_scale, up_scale, partners, latent_in, latent_out
):
    tok_rows = tokens.shape[0]
    blocks, slot_count, part_rows, blk_width = gate_weight.shape
    feat_count = lax.axis_size("feat")
    chips = lax.axis_size("tok") // PAIR
    half = chips // 2
    local_bits = blocks.bit_length() - 1
    feat_bits = feat_count.bit_length() - 1
    place = lax.axis_index("tok")
    chip, lane = place // PAIR, place % PAIR
    on_right = chip >= half
    distance = jnp.where(on_right, chip - half, half - 1 - chip)
    inward = [[(half - 1 - q, half - 1), (half + q, half)] for q in range(half)]
    across = [[(half - 1 - q, half), (half + q, half - 1)] for q in range(half)]
    outward = [[(half - 1, half - 1 - q), (half, half + q)] for q in range(half)]

    first_block = lax.axis_index("feat") * blocks
    block_ids = first_block + jnp.arange(blocks, dtype=jnp.int32)
    offsets = [0] + [1 << bit_pos for bit_pos in range(local_bits + feat_bits)]
    labels = jnp.bitwise_xor(block_ids[:, None], jnp.array(offsets, dtype=jnp.int32)[None, :])
    wanted = lax.dynamic_slice_in_dim(partners, first_block, blocks, 0)
    matched = wanted[:, :, None] == labels[:, None, :]
    slot_ids = jnp.arange(slot_count, dtype=jnp.int32)
    slots = jnp.sum(jnp.where(matched, slot_ids[None, :, None], 0), axis=1)
    ready = [
        joined_weights(slots, gate_weight, up_weight, gate_scale, up_scale, own_block)
        for own_block in range(blocks)
    ]

    pieces = tokens.T.reshape(blocks, chips, PAIR, part_rows, tok_rows).transpose(2, 1, 0, 3, 4)
    pieces = jnp.where(lane == 0, pieces, pieces[::-1])
    left, right = pieces[:, :half][:, ::-1], pieces[:, half:]
    near = jnp.where(on_right, right, left)
    far = jnp.where(on_right, left, right)
    step = part_blocks(blocks)
    far_parts = [far[:, :, start : start + step] for start in range(0, blocks, step)]
    from_far = [[moved(part, across[q]) for part in far_parts] for q in range(half)]
    from_near = [[near]] + [[moved(near, inward[q])] for q in range(1, half)]
    shipped = [
        [ready[block]]
        + [moved(ready[block], inward[q]) for q in range(1, half)]
        for block in range(blocks)
    ]

    def turned(groups):
        return [
            [[swapped(value, "feat", bit) for value in parts] for bit in range(feat_bits)]
            for parts in groups
        ]

    far_remote = turned(from_far)
    near_remote = turned(from_near)

    def block_of(parts, block):
        size = blocks // len(parts)
        return parts[block // size][:, :, block % size]

    def inputs_of(own_block, groups, remotes):
        rows = []
        for group, remote in zip(groups, remotes):
            picked = [block_of(group, own_block)]
            for bit_pos in range(local_bits):
                picked.append(block_of(group, own_block ^ 1 << bit_pos))
            for bit_pos in range(feat_bits):
                picked.append(block_of(remote[bit_pos], own_block))
            rows.append(jnp.stack(picked, axis=2).reshape(-1, tok_rows))
        return jnp.concatenate(rows, axis=1)

    def product(inputs, weights):
        return lax.dot_general(
            inputs, weights, (((0,), (0,)), ((), ())), preferred_element_type=jnp.float32
        )

    latent_part = jnp.zeros((tok_rows, latent_in.shape[1]), jnp.float32)
    hidden = []
    for own_block in range(blocks):
        mine = jnp.concatenate(shipped[own_block], axis=0)
        other = swapped(mine, "tok", 0)
        weights = jnp.concatenate([mine, other], axis=0).reshape(-1, 2 * blk_width)
        inputs = inputs_of(own_block, from_far, far_remote)
        away = product(inputs, weights).astype(jnp.bfloat16)
        back = moved(away, across[0])
        inputs = inputs_of(own_block, from_near, near_remote)
        home = product(inputs, weights)
        sums = home + back.astype(jnp.float32)
        done = (jax.nn.silu(sums[:, :blk_width]) * sums[:, blk_width:]).astype(jnp.bfloat16)
        block_hidden = done[:tok_rows]
        for q in range(1, half):
            share = done[q * tok_rows : (q + 1) * tok_rows]
            sent = moved(share, outward[q])
            block_hidden = jnp.where(distance == q, sent, block_hidden)
        hidden.append(block_hidden)
        rows = latent_in[own_block * blk_width : (own_block + 1) * blk_width]
        latent_part += jnp.dot(block_hidden, rows, preferred_element_type=jnp.float32)
    latent = latent_part
    for bit_pos in range(feat_bits):
        share = latent.astype(jnp.bfloat16)
        latent = share.astype(jnp.float32) + swapped(share, "feat", bit_pos).astype(jnp.float32)
    latent = latent.astype(jnp.bfloat16)
    rank_term = jnp.dot(latent, latent_out, preferred_element_type=jnp.float32).astype(jnp.bfloat16)
    return (jnp.concatenate(hidden, axis=1), rank_term)


MESH = pl.DeviceIdType.MESH
VMEM_BYTES = 64 * 2**20


def flipped(value, bit):
    mask = 2**bit
    return value + mask - 2 * mask * ((value // mask) % 2)


class Sends:
    def __init__(self):
        self.started = []

    def start(self, copy):
        copy.start()
        self.started.append(copy)

    def drain(self):
        for copy in self.started:
            copy.wait_send()


def hidden_kernel(
    half, feat_bits, partners, gate_scale, up_scale, tokens, gate, up, hidden, *scratch
):
    blocks, slot_count, part_rows, width = gate.shape
    rows = tokens.shape[0]
    parts = PAIR * half
    depth = parts * part_rows
    chunks = 2 * blocks
    local_bits = blocks.bit_length() - 1
    tile = math.gcd(width, 256)
    weights, scratch = scratch[:chunks], scratch[chunks:]
    far_x, near_x, sent, got, early, made, *semaphores = scratch
    (
        far_out, far_land, near_out, near_land, near_own,
        turn_far_out, turn_far_land, turn_near_out, turn_near_land,
        weight_out, weight_land, lane_out, lane_land, weight_own,
        sum_out, sum_land, give_out, give_land, keep_own,
    ) = semaphores

    feat = lax.axis_index("feat")
    tok = lax.axis_index("tok")
    lane, chip = tok % PAIR, tok // PAIR
    side = chip // half
    distance = side * (chip - half) + (1 - side) * (half - 1 - chip)
    part = tok - side * parts
    middle = (half - 1 + side) * PAIR + lane
    across = (half - side) * PAIR + lane
    partner = tok + 1 - 2 * lane

    def chip_of(which, q):
        return which * (half + q) + (1 - which) * (half - 1 - q)

    def part_of(q, which_lane):
        return (chip_of(side, q) - side * half) * PAIR + which_lane

    def remote(source, target, out, land, **where):
        return pltpu.make_async_remote_copy(
            src_ref=source,
            dst_ref=target,
            send_sem=out,
            recv_sem=land,
            device_id=where,
            device_id_type=MESH,
        )

    def columns(block, which):
        return pl.ds(pl.multiple_of(block * width + which * depth, math.gcd(width, depth)), depth)

    def far_copy(q, block, target):
        source = tokens.at[:, columns(block, 1 - side)]
        return remote(source, far_x.at[block, q], far_out.at[block], far_land.at[q, block], tok=target)

    def near_copy(q, block, target):
        source = tokens.at[:, columns(block, side)]
        return remote(source, near_x.at[block, q], near_out.at[block], near_land.at[q, block], tok=target)

    def stored(chunk):
        return (gate, up)[chunk % 2].at[chunk // 2]

    def weight_copy(q, chunk, target):
        place = weights[chunk].at[:, part_of(q, lane)]
        return remote(stored(chunk), place, weight_out.at[chunk], weight_land.at[q, chunk], tok=target)

    def give_copy(q, block, target):
        place = hidden.at[:, pl.ds(block * width, width)]
        return remote(made.at[block, q], place, give_out.at[q, block], give_land.at[block], tok=target)

    barrier = pltpu.get_barrier_semaphore()

    def greet(count, peers):
        for peer in peers:
            pl.semaphore_signal(barrier, inc=1, device_id=peer, device_id_type=MESH)
        pl.semaphore_wait(barrier, count)

    def outer(q):
        greet(2, [{"tok": middle}, {"tok": across}])
        sends = Sends()
        nears = list(range(blocks))
        sends.start(weight_copy(q, 0, middle))
        for block in range(blocks):
            sends.start(far_copy(q, block, across))
        for chunk in range(1, chunks):
            sends.start(weight_copy(q, chunk, middle))
            if nears:
                sends.start(near_copy(q, nears.pop(0), middle))
        for block in nears:
            sends.start(near_copy(q, block, middle))
        for block in range(blocks):
            give_copy(q, block, middle).wait_recv()
        sends.drain()

    def inner():
        peers = [{"tok": partner}, {"tok": across}]
        for q in range(1, half):
            peers += [{"tok": chip_of(which, q) * PAIR + lane} for which in (side, 1 - side)]
        peers += [{"feat": flipped(feat, bit)} for bit in range(feat_bits)]
        greet(len(peers), peers)
        sends = Sends()
        own = []

        for block in range(blocks):
            sends.start(far_copy(0, block, across))
        for chunk in range(chunks):
            place = weights[chunk].at[:, part]
            copy = remote(stored(chunk), place, lane_out.at[0, chunk], lane_land.at[0, chunk], tok=partner)
            sends.start(copy)
            copy = pltpu.make_async_copy(stored(chunk), place, weight_own.at[chunk])
            copy.start()
            own.append(copy)
        near_copies = []
        for block in range(blocks):
            source = tokens.at[:, columns(block, side)]
            copy = pltpu.make_async_copy(source, near_x.at[block, 0], near_own.at[block])
            copy.start()
            near_copies.append(copy)

        def turn(x, q, block, out, land):
            for bit in range(feat_bits):
                place = x.at[blocks * (1 + bit) + block, q]
                sends.start(
                    remote(
                        x.at[block, q], place, out.at[bit, q, block], land.at[bit, q, block],
                        feat=flipped(feat, bit),
                    )
                )

        def turned(x, block, out, land):
            for q in range(half):
                for bit in range(feat_bits):
                    place = x.at[blocks * (1 + bit) + block, q]
                    remote(
                        x.at[block, q], place, out.at[bit, q, block], land.at[bit, q, block],
                        feat=flipped(feat, bit),
                    ).wait_recv()

        def take_far(q):
            for block in range(blocks):
                far_copy(q, block, across).wait_recv()
                turn(far_x, q, block, turn_far_out, turn_far_land)

        def take_near(q, block):
            near_copy(q, block, middle).wait_recv()
            turn(near_x, q, block, turn_near_out, turn_near_land)

        def take_weights(chunk):
            for q in range(1, half):
                weight_copy(q, chunk, middle).wait_recv()
                place = weights[chunk].at[:, part_of(q, lane)]
                sends.start(
                    remote(place, place, lane_out.at[q, chunk], lane_land.at[q, chunk], tok=partner)
                )

        def whole_weights(chunk):
            own[chunk].wait()
            for q in range(half):
                place = weights[chunk].at[:, part_of(q, 1 - lane)]
                remote(
                    place, place, lane_out.at[q, chunk], lane_land.at[q, chunk], tok=partner
                ).wait_recv()

        def slots_of(block):
            row = feat * blocks + block
            found = []
            for offset in [0] + [2**bit for bit in range(local_bits + feat_bits)]:
                label = jnp.bitwise_xor(row, offset)
                slot = jnp.int32(0)
                for k in range(1, slot_count):
                    slot = jnp.where(partners[row, k] == label, k, slot)
                found.append(slot)
            return found

        slots = [slots_of(block) for block in range(blocks)]

        def sums(x, chunk, cols):
            block = chunk // 2
            scale = (gate_scale, up_scale)[chunk % 2]
            places = [block] + [block ^ 2**bit for bit in range(local_bits)]
            places += [blocks * (1 + bit) + block for bit in range(feat_bits)]
            total = None
            for place, slot in zip(places, slots[block]):
                inputs = x[place].reshape(half * rows, depth)
                weight = weights[chunk][slot, :, :, cols].reshape(depth, tile)
                term = jnp.dot(inputs, weight, preferred_element_type=jnp.float32)
                term = term * scale[block, slot]
                total = term if total is None else total + term
            return total

        def tiles(body):
            @pl.loop(0, width // tile)
            def _(step):
                body(pl.ds(pl.multiple_of(step * tile, tile), tile))

        def sum_copy(chunk):
            return remote(sent.at[chunk], got.at[chunk], sum_out.at[chunk], sum_land.at[chunk], tok=across)

        def away(chunk):
            whole_weights(chunk)

            def body(cols):
                value = sums(far_x, chunk, cols)
                sent[chunk, :, :, cols] = value.astype(sent.dtype).reshape(half, rows, tile)

            tiles(body)
            sends.start(sum_copy(chunk))

        def joined(value, chunk, cols):
            return value + got[chunk, :, :, cols].reshape(half * rows, tile).astype(jnp.float32)

        def finish(block, first, second):
            for chunk in (2 * block, 2 * block + 1):
                sum_copy(chunk).wait_recv()

            def body(cols):
                gated = joined(first(cols), 2 * block, cols)
                raised = joined(second(cols), 2 * block + 1, cols)
                value = gated / (1.0 + jnp.exp(-gated)) * raised
                made[block, :, :, cols] = value.astype(made.dtype).reshape(half, rows, tile)

            tiles(body)
            for q in range(1, half):
                sends.start(give_copy(q, block, chip_of(side, q) * PAIR + lane))
            copy = pltpu.make_async_copy(
                made.at[block, 0], hidden.at[:, pl.ds(block * width, width)], keep_own.at[block]
            )
            copy.start()
            return copy

        def home(block):
            turned(near_x, block, turn_near_out, turn_near_land)
            return finish(
                block,
                lambda cols: sums(near_x, 2 * block, cols),
                lambda cols: sums(near_x, 2 * block + 1, cols),
            )

        take_far(0)
        take_weights(0)
        for q in range(1, half):
            take_far(q)
        for block in range(blocks):
            near_copies[block].wait()
            turn(near_x, 0, block, turn_near_out, turn_near_land)
        nears = list(range(blocks))
        homes = list(range(blocks - 1))
        kept = []
        for chunk in range(chunks):
            if chunk:
                take_weights(chunk)
            if chunk % 2 == 0:
                turned(far_x, chunk // 2, turn_far_out, turn_far_land)
            away(chunk)
            if chunk and nears:
                block = nears.pop(0)
                for q in range(1, half):
                    take_near(q, block)
            if not nears and homes and 2 * homes[0] + 4 <= chunk:
                kept.append(home(homes.pop(0)))
        for block in nears:
            for q in range(1, half):
                take_near(q, block)
        for block in homes:
            kept.append(home(block))
        last = blocks - 1
        turned(near_x, last, turn_near_out, turn_near_land)

        def body(cols):
            for kind in range(2):
                early[kind, :, cols] = sums(near_x, 2 * last + kind, cols)

        tiles(body)
        kept.append(
            finish(last, lambda cols: early[0, :, cols], lambda cols: early[1, :, cols])
        )
        for copy in kept:
            copy.wait()
        sends.drain()

    for q in range(1, half):
        pl.when(distance == q)(lambda q=q: outer(q))
    pl.when(distance == 0)(inner)


def kernel_scratch(half, feat_bits, rows, weight_shape):
    blocks, slot_count, part_rows, width = weight_shape
    chunks = 2 * blocks
    parts = PAIR * half
    sources = blocks * (1 + feat_bits)
    depth = parts * part_rows
    low = jnp.bfloat16
    arrays = [((slot_count, parts, part_rows, width), low)] * chunks
    arrays += [((sources, half, rows, depth), low)] * 2
    arrays += [((chunks, half, rows, width), low)] * 2
    arrays += [((2, half * rows, width), jnp.float32)]
    arrays += [((blocks, half, rows, width), low)]
    counts = [
        (blocks,), (half, blocks), (blocks,), (half, blocks), (blocks,),
        (feat_bits, half, blocks), (feat_bits, half, blocks),
        (feat_bits, half, blocks), (feat_bits, half, blocks),
        (chunks,), (half, chunks), (half, chunks), (half, chunks), (chunks,),
        (chunks,), (chunks,), (half, blocks), (blocks,), (blocks,),
    ]
    return arrays, counts


def kernel_fits(half, feat_bits, rows, weight_shape):
    arrays, _ = kernel_scratch(half, feat_bits, rows, weight_shape)
    size = sum(math.prod(shape) * jnp.dtype(kind).itemsize for shape, kind in arrays)
    return half > 1 and size <= VMEM_BYTES * 7 // 8


def hidden_of(tokens, gate_weight, up_weight, gate_scale, up_scale, partners):
    half = lax.axis_size("tok") // PAIR // 2
    feat_bits = lax.axis_size("feat").bit_length() - 1
    arrays, counts = kernel_scratch(half, feat_bits, tokens.shape[0], gate_weight.shape)
    scalars = pl.BlockSpec(memory_space=pltpu.SMEM)
    whole = pl.BlockSpec(memory_space=pl.ANY)
    return pl.pallas_call(
        functools.partial(hidden_kernel, half, feat_bits),
        out_shape=jax.ShapeDtypeStruct(tokens.shape, jnp.bfloat16),
        in_specs=[scalars] * 3 + [whole] * 3,
        out_specs=whole,
        scratch_shapes=[pltpu.VMEM(*one) for one in arrays]
        + [pltpu.SemaphoreType.DMA(count) for count in counts],
        compiler_params=pltpu.CompilerParams(
            collective_id=0, has_side_effects=True, vmem_limit_bytes=VMEM_BYTES - 2**17
        ),
        name="hidden",
    )(partners, gate_scale, up_scale, tokens, gate_weight, up_weight)


def fused(tokens, gate_weight, up_weight, gate_scale, up_scale, partners, latent_in, latent_out):
    feat_bits = lax.axis_size("feat").bit_length() - 1
    hidden = hidden_of(tokens, gate_weight, up_weight, gate_scale, up_scale, partners)
    latent = jnp.dot(hidden, latent_in, preferred_element_type=jnp.float32)
    for bit_pos in range(feat_bits):
        share = latent.astype(jnp.bfloat16)
        latent = share.astype(jnp.float32) + swapped(share, "feat", bit_pos).astype(jnp.float32)
    latent = latent.astype(jnp.bfloat16)
    rank_term = jnp.dot(latent, latent_out, preferred_element_type=jnp.float32).astype(jnp.bfloat16)
    return hidden, rank_term


def solution(mesh):
    placed = (
        P("tok", "feat"),
        P("feat", None, "tok", None),
        P("feat", None, "tok", None),
        P("feat", None),
        P("feat", None),
        P(),
        P("feat", None),
        P(None, "feat"),
    )
    feat_bits = mesh.shape["feat"].bit_length() - 1
    half = mesh.shape["tok"] // PAIR // 2

    def sharded(function):
        return jax.shard_map(
            function,
            mesh=mesh,
            in_specs=placed,
            out_specs=(P("tok", "feat"), P("tok", "feat")),
            check_vma=False,
        )

    def run(*args):
        rows = args[0].shape[0] // mesh.shape["tok"]
        blocks, slot_count, depth, width = args[1].shape
        blocks //= mesh.shape["feat"]
        local = (blocks, slot_count, depth // mesh.shape["tok"], width)
        if kernel_fits(half, feat_bits, rows, local):
            return sharded(fused)(*args)
        return sharded(per_device)(*args)

    return run
```

```python
import functools
import math

import jax
import jax.numpy as jnp
from jax import lax
from jax.experimental import pallas as pl
from jax.experimental.pallas import tpu as pltpu
from jax.sharding import PartitionSpec as P


PAIR = 2


def swapped(value, axis, bit):
    mask = 2**bit
    pairs = [(source, source ^ mask) for source in range(lax.axis_size(axis))]
    return lax.ppermute(value, axis, pairs)


def moved(value, chip_pairs):
    pairs = [
        (PAIR * source + lane, PAIR * target + lane)
        for source, target in chip_pairs
        for lane in range(PAIR)
    ]
    return lax.ppermute(value, "tok", pairs)


def join_kernel(slots, gate, up, gate_scale, up_scale, joined, *, block):
    slot = slots[block, pl.program_id(0)]
    width = gate.shape[-1]
    for start, weight, scale in ((0, gate, gate_scale), (width, up, up_scale)):
        product = weight[0, 0].astype(jnp.float32) * scale[block, slot]
        joined[0, :, start : start + width] = product.astype(joined.dtype)


def joined_weights(slots, gate_weight, up_weight, gate_scale, up_scale, block):
    _, slot_count, rows, width = gate_weight.shape
    picked = pl.BlockSpec((1, 1, rows, width), lambda k, slots: (block, slots[block, k], 0, 0))
    whole = pl.BlockSpec(memory_space=pltpu.SMEM)
    size = slot_count * rows * width
    return pl.pallas_call(
        lambda *refs: join_kernel(*refs, block=block),
        out_shape=jax.ShapeDtypeStruct((slot_count, rows, 2 * width), jnp.bfloat16),
        grid_spec=pltpu.PrefetchScalarGridSpec(
            num_scalar_prefetch=1,
            grid=(slot_count,),
            in_specs=[picked, picked, whole, whole],
            out_specs=pl.BlockSpec((1, rows, 2 * width), lambda k, slots: (k, 0, 0)),
        ),
        cost_estimate=pl.CostEstimate(flops=2 * size, bytes_accessed=8 * size, transcendentals=0),
    )(slots, gate_weight, up_weight, gate_scale, up_scale)


def part_blocks(blocks):
    return max(1, blocks // 2)


def per_device(
    tokens, gate_weight, up_weight, gate_scale, up_scale, partners, latent_in, latent_out
):
    tok_rows = tokens.shape[0]
    blocks, slot_count, part_rows, blk_width = gate_weight.shape
    feat_count = lax.axis_size("feat")
    chips = lax.axis_size("tok") // PAIR
    half = chips // 2
    local_bits = blocks.bit_length() - 1
    feat_bits = feat_count.bit_length() - 1
    place = lax.axis_index("tok")
    chip, lane = place // PAIR, place % PAIR
    on_right = chip >= half
    distance = jnp.where(on_right, chip - half, half - 1 - chip)
    inward = [[(half - 1 - q, half - 1), (half + q, half)] for q in range(half)]
    across = [[(half - 1 - q, half), (half + q, half - 1)] for q in range(half)]
    outward = [[(half - 1, half - 1 - q), (half, half + q)] for q in range(half)]

    first_block = lax.axis_index("feat") * blocks
    block_ids = first_block + jnp.arange(blocks, dtype=jnp.int32)
    offsets = [0] + [1 << bit_pos for bit_pos in range(local_bits + feat_bits)]
    labels = jnp.bitwise_xor(block_ids[:, None], jnp.array(offsets, dtype=jnp.int32)[None, :])
    wanted = lax.dynamic_slice_in_dim(partners, first_block, blocks, 0)
    matched = wanted[:, :, None] == labels[:, None, :]
    slot_ids = jnp.arange(slot_count, dtype=jnp.int32)
    slots = jnp.sum(jnp.where(matched, slot_ids[None, :, None], 0), axis=1)
    ready = [
        joined_weights(slots, gate_weight, up_weight, gate_scale, up_scale, own_block)
        for own_block in range(blocks)
    ]

    pieces = tokens.T.reshape(blocks, chips, PAIR, part_rows, tok_rows).transpose(2, 1, 0, 3, 4)
    pieces = jnp.where(lane == 0, pieces, pieces[::-1])
    left, right = pieces[:, :half][:, ::-1], pieces[:, half:]
    near = jnp.where(on_right, right, left)
    far = jnp.where(on_right, left, right)
    step = part_blocks(blocks)
    far_parts = [far[:, :, start : start + step] for start in range(0, blocks, step)]
    from_far = [[moved(part, across[q]) for part in far_parts] for q in range(half)]
    from_near = [[near]] + [[moved(near, inward[q])] for q in range(1, half)]
    shipped = [
        [ready[block]]
        + [moved(ready[block], inward[q]) for q in range(1, half)]
        for block in range(blocks)
    ]

    def turned(groups):
        return [
            [[swapped(value, "feat", bit) for value in parts] for bit in range(feat_bits)]
            for parts in groups
        ]

    far_remote = turned(from_far)
    near_remote = turned(from_near)

    def block_of(parts, block):
        size = blocks // len(parts)
        return parts[block // size][:, :, block % size]

    def inputs_of(own_block, groups, remotes):
        rows = []
        for group, remote in zip(groups, remotes):
            picked = [block_of(group, own_block)]
            for bit_pos in range(local_bits):
                picked.append(block_of(group, own_block ^ 1 << bit_pos))
            for bit_pos in range(feat_bits):
                picked.append(block_of(remote[bit_pos], own_block))
            rows.append(jnp.stack(picked, axis=2).reshape(-1, tok_rows))
        return jnp.concatenate(rows, axis=1)

    def product(inputs, weights):
        return lax.dot_general(
            inputs, weights, (((0,), (0,)), ((), ())), preferred_element_type=jnp.float32
        )

    latent_part = jnp.zeros((tok_rows, latent_in.shape[1]), jnp.float32)
    hidden = []
    for own_block in range(blocks):
        mine = jnp.concatenate(shipped[own_block], axis=0)
        other = swapped(mine, "tok", 0)
        weights = jnp.concatenate([mine, other], axis=0).reshape(-1, 2 * blk_width)
        inputs = inputs_of(own_block, from_far, far_remote)
        away = product(inputs, weights).astype(jnp.bfloat16)
        back = moved(away, across[0])
        inputs = inputs_of(own_block, from_near, near_remote)
        home = product(inputs, weights)
        sums = home + back.astype(jnp.float32)
        done = (jax.nn.silu(sums[:, :blk_width]) * sums[:, blk_width:]).astype(jnp.bfloat16)
        block_hidden = done[:tok_rows]
        for q in range(1, half):
            share = done[q * tok_rows : (q + 1) * tok_rows]
            sent = moved(share, outward[q])
            block_hidden = jnp.where(distance == q, sent, block_hidden)
        hidden.append(block_hidden)
        rows = latent_in[own_block * blk_width : (own_block + 1) * blk_width]
        latent_part += jnp.dot(block_hidden, rows, preferred_element_type=jnp.float32)
    latent = latent_part
    for bit_pos in range(feat_bits):
        share = latent.astype(jnp.bfloat16)
        latent = share.astype(jnp.float32) + swapped(share, "feat", bit_pos).astype(jnp.float32)
    latent = latent.astype(jnp.bfloat16)
    rank_term = jnp.dot(latent, latent_out, preferred_element_type=jnp.float32).astype(jnp.bfloat16)
    return (jnp.concatenate(hidden, axis=1), rank_term)


MESH = pl.DeviceIdType.MESH
VMEM_BYTES = 64 * 2**20
TILE = 256


def flipped(value, bit):
    mask = 2**bit
    return value + mask - 2 * mask * ((value // mask) % 2)


def hidden_kernel(
    half, feat_bits, partners, gate_scale, up_scale, tokens, gate, up, latent_in,
    hidden, latent, *scratch
):
    blocks, slot_count, part_rows, width = gate.shape
    rows = tokens.shape[0]
    parts = PAIR * half
    depth = parts * part_rows
    tile = math.gcd(width, TILE)
    cuts = width // tile
    steps = 2 * blocks * cuts
    pieces = blocks * cuts
    (
        weights, far_x, near_x, sent, got, early, made, factor, total, share, shared,
        far_out, far_land, near_out, near_land, near_own,
        turn_far_out, turn_far_land, turn_near_out, turn_near_land,
        weight_out, weight_land, lane_out, lane_land, weight_own,
        sum_out, sum_land, give_out, give_land, keep_own, factor_own, share_out, share_land,
    ) = scratch

    feat = lax.axis_index("feat")
    tok = lax.axis_index("tok")
    lane, chip = tok % PAIR, tok // PAIR
    side = chip // half
    distance = side * (chip - half) + (1 - side) * (half - 1 - chip)
    middle = (half - 1 + side) * PAIR + lane
    across = (half - side) * PAIR + lane
    partner = tok + 1 - 2 * lane

    def chip_of(which, q):
        return which * (half + q) + (1 - which) * (half - 1 - q)

    def tok_of(which, q):
        return chip_of(which, q) * PAIR + lane

    def part_of(q, which_lane):
        return (chip_of(side, q) - side * half) * PAIR + which_lane

    def remote(source, target, out, land, **where):
        return pltpu.make_async_remote_copy(
            src_ref=source,
            dst_ref=target,
            send_sem=out,
            recv_sem=land,
            device_id=where,
            device_id_type=MESH,
        )

    def columns(block, which):
        return pl.ds(pl.multiple_of(block * width + which * depth, math.gcd(width, depth)), depth)

    def far_copy(q, block, target):
        source = tokens.at[:, columns(block, 1 - side)]
        return remote(source, far_x.at[block, q], far_out.at[block], far_land.at[q, block], tok=target)

    def near_copy(q, block, target):
        source = tokens.at[:, columns(block, side)]
        return remote(source, near_x.at[block, q], near_out.at[block], near_land.at[q, block], tok=target)

    def turn_copy(x, q, block, bit, out, land):
        place = x.at[blocks * (1 + bit) + block, q]
        semaphores = out.at[bit, q, block], land.at[bit, q, block]
        return remote(x.at[block, q], place, *semaphores, feat=flipped(feat, bit))

    def stored(step):
        block, kind, cut = step // (2 * cuts), step // cuts % 2, step % cuts
        return (gate, up)[kind].at[block, :, :, pl.ds(cut * tile, tile)]

    def weight_copy(q, step, source, target):
        place = weights.at[step, :, part_of(q, lane)]
        return remote(source, place, weight_out.at[step], weight_land.at[q, step], tok=target)

    def lane_copy(q, step, source, which_lane):
        place = weights.at[step, :, part_of(q, which_lane)]
        source = place if source is None else source
        return remote(source, place, lane_out.at[q, step], lane_land.at[q, step], tok=partner)

    def own_copy(step, source):
        return pltpu.make_async_copy(
            source, weights.at[step, :, part_of(0, lane)], weight_own.at[step]
        )

    def sum_copy(q, step):
        return remote(sent.at[step, q], got.at[step, q], sum_out.at[q, step], sum_land.at[q, step], tok=across)

    def give_copy(q, piece, target):
        return remote(made.at[piece, q], made.at[piece, 0], give_out.at[q, piece], give_land.at[piece], tok=target)

    def keep_copy(piece):
        place = hidden.at[:, pl.ds(pl.multiple_of(piece * tile, tile), tile)]
        return pltpu.make_async_copy(made.at[piece, 0], place, keep_own.at[piece])

    def share_copy(stage, part):
        bit = (stage + part) % feat_bits
        semaphores = share_out.at[stage, part], share_land.at[stage, part]
        return remote(share.at[stage, part], shared.at[stage, part], *semaphores, feat=flipped(feat, bit))

    factor_copy = pltpu.make_async_copy(latent_in, factor, factor_own)
    factor_copy.start()
    barrier = pltpu.get_barrier_semaphore()

    def greet(peers):
        for peer in peers:
            pl.semaphore_signal(barrier, inc=1, device_id=peer, device_id_type=MESH)
        pl.semaphore_wait(barrier, len(peers))

    turns = [{"feat": flipped(feat, bit)} for bit in range(feat_bits)]

    def project(piece):
        total[...] += jnp.dot(
            made[piece, 0], factor[piece], preferred_element_type=jnp.float32
        )

    def clear():
        factor_copy.wait()
        total[...] = jnp.zeros_like(total)

    def near_after(block):
        return min(2 * cuts - 1 + 2 * block, steps - 1)

    first_home = max(near_after(blocks - 1) + 2, steps - 1 - (pieces - cuts))
    assert first_home < steps

    def outer(q):
        greet([{"tok": middle}, {"tok": across}] + turns)
        for step in range(cuts):
            weight_copy(q, step, stored(step), middle).start()
        for block in range(blocks):
            far_copy(q, block, across).start()
        for step in range(cuts, steps):
            weight_copy(q, step, stored(step), middle).start()
            for block in range(blocks):
                if near_after(block) == step:
                    near_copy(q, block, middle).start()
        clear()

        @pl.loop(0, pieces)
        def _(piece):
            give_copy(q, piece, middle).wait_recv()
            keep_copy(piece).start()
            project(piece)

        for block in range(blocks):
            far_copy(q, block, across).wait_send()
            near_copy(q, block, middle).wait_send()

        for step in range(steps):
            weight_copy(q, step, stored(step), middle).wait_send()

    def inner():
        peers = [{"tok": partner}, {"tok": across}]
        for q in range(1, half):
            peers += [{"tok": tok_of(which, q)} for which in (side, 1 - side)]
        greet(peers + turns)
        for block in range(blocks):
            far_copy(0, block, across).start()
        for step in range(steps):
            lane_copy(0, step, stored(step), lane).start()
            own_copy(step, stored(step)).start()
        near_own_copies = []
        for block in range(blocks):
            source = tokens.at[:, columns(block, side)]
            copy = pltpu.make_async_copy(source, near_x.at[block, 0], near_own.at[block])
            copy.start()
            near_own_copies.append(copy)

        far_turn = (turn_far_out, turn_far_land)
        near_turn = (turn_near_out, turn_near_land)

        def every_turn(x, semaphores, act):
            for block in range(blocks):
                for q in range(half):
                    for bit in range(feat_bits):
                        act(turn_copy(x, q, block, bit, *semaphores))

        for block in range(blocks):
            for q in range(half):
                far_copy(q, block, across).wait_recv()
                for bit in range(feat_bits):
                    turn_copy(far_x, q, block, bit, *far_turn).start()
        for block in range(blocks):
            near_own_copies[block].wait()
            for bit in range(feat_bits):
                turn_copy(near_x, 0, block, bit, *near_turn).start()
        clear()
        every_turn(far_x, far_turn, lambda copy: copy.wait_recv())

        def source_of(block, slot):
            row = feat * blocks + block
            label = partners[row, slot]
            place = label % blocks
            for bit in range(feat_bits):
                other = flipped(feat, bit) * blocks + block
                place = jnp.where(label == other, blocks * (1 + bit) + block, place)
            return place

        def sums(x, step):
            block, kind = step // (2 * cuts), step // cuts % 2
            value = None
            for slot in range(slot_count):
                scale = jnp.where(kind == 0, gate_scale[block, slot], up_scale[block, slot])
                inputs = x[source_of(block, slot)].reshape(half * rows, depth)
                weight = weights[step, slot].reshape(depth, tile)
                term = jnp.dot(inputs, weight, preferred_element_type=jnp.float32) * scale
                value = term if value is None else value + term
            return value

        def pair_of(piece):
            step = piece // cuts * 2 * cuts + piece % cuts
            return step, step + cuts

        def gated(first, second):
            return (first / (1.0 + jnp.exp(-first)) * second).astype(made.dtype)

        def home(piece):
            for q in range(half):
                for step in pair_of(piece):
                    sum_copy(q, step).wait_recv()
            first, second = [
                sums(near_x, step) + got[step].reshape(half * rows, tile).astype(jnp.float32)
                for step in pair_of(piece)
            ]
            made[piece] = gated(first, second).reshape(half, rows, tile)
            for q in range(1, half):
                give_copy(q, piece, tok_of(side, q)).start()
            keep_copy(piece).start()
            project(piece)

        @pl.loop(0, steps)
        def _(step):
            for q in range(1, half):
                weight_copy(q, step, stored(0), middle).wait_recv()
                lane_copy(q, step, None, lane).start()
            own_copy(step, stored(0)).wait()
            for q in range(half):
                lane_copy(q, step, None, 1 - lane).wait_recv()
            sent[step] = sums(far_x, step).astype(sent.dtype).reshape(half, rows, tile)
            for q in reversed(range(half)):
                sum_copy(q, step).start()
            for block in range(blocks):

                @pl.when(step == near_after(block))
                def _():
                    for q in range(1, half):
                        near_copy(q, block, middle).wait_recv()
                        for bit in range(feat_bits):
                            turn_copy(near_x, q, block, bit, *near_turn).start()

            @pl.when(step == first_home)
            def _():
                every_turn(near_x, near_turn, lambda copy: copy.wait_recv())

            @pl.when((step >= first_home) & (step < first_home + pieces - cuts))
            def _():
                home(step - first_home)

        @pl.loop(steps, first_home + pieces - cuts)
        def _(step):
            home(step - first_home)

        @pl.loop(0, cuts)
        def _(cut):
            for kind, step in enumerate(pair_of(pieces - cuts + cut)):
                early[kind, cut] = sums(near_x, step).reshape(half, rows, tile)

        @pl.loop(0, cuts)
        def _(cut):
            piece = pieces - cuts + cut
            for q in reversed(range(half)):
                values = []
                for kind, step in enumerate(pair_of(piece)):
                    sum_copy(q, step).wait_recv()
                    values.append(early[kind, cut, q] + got[step, q].astype(jnp.float32))
                made[piece, q] = gated(*values)
                if q:
                    give_copy(q, piece, tok_of(side, q)).start()
            keep_copy(piece).start()
            project(piece)

    for q in range(1, half):
        pl.when(distance == q)(lambda q=q: outer(q))
    pl.when(distance == 0)(inner)

    part_width = total.shape[1] // feat_bits
    for stage in range(feat_bits):
        for part in range(feat_bits):
            span = pl.ds(part * part_width, part_width)
            share[stage, part] = total[:, span].astype(share.dtype)
            share_copy(stage, part).start()
        for part in range(feat_bits):
            span = pl.ds(part * part_width, part_width)
            share_copy(stage, part).wait_recv()
            ours = share[stage, part].astype(jnp.float32)
            total[:, span] = ours + shared[stage, part].astype(jnp.float32)
    latent[...] = total[...].astype(latent.dtype)

    @pl.loop(0, pieces)
    def _(piece):
        keep_copy(piece).wait()

    for stage in range(feat_bits):
        for part in range(feat_bits):
            share_copy(stage, part).wait_send()

    @pl.when(distance == 0)
    def _():
        for block in range(blocks):
            far_copy(0, block, across).wait_send()
            for q in range(half):
                for bit in range(feat_bits):
                    turn_copy(far_x, q, block, bit, turn_far_out, turn_far_land).wait_send()
                    turn_copy(near_x, q, block, bit, turn_near_out, turn_near_land).wait_send()

        @pl.loop(0, steps)
        def _(step):
            for q in range(half):
                lane_copy(q, step, None, lane).wait_send()
                sum_copy(q, step).wait_send()

        @pl.loop(0, pieces)
        def _(piece):
            for q in range(1, half):
                give_copy(q, piece, tok_of(side, q)).wait_send()


def kernel_scratch(half, feat_bits, rows, weight_shape, rank):
    blocks, slot_count, part_rows, width = weight_shape
    tile = math.gcd(width, TILE)
    cuts = width // tile
    steps, pieces = 2 * blocks * cuts, blocks * cuts
    parts = PAIR * half
    sources = blocks * (1 + feat_bits)
    depth = parts * part_rows
    low, high = jnp.bfloat16, jnp.float32
    arrays = [
        ((steps, slot_count, parts, part_rows, tile), low),
        ((sources, half, rows, depth), low),
        ((sources, half, rows, depth), low),
        ((steps, half, rows, tile), low),
        ((steps, half, rows, tile), low),
        ((2, cuts, half, rows, tile), high),
        ((pieces, half, rows, tile), low),
        ((pieces, tile, rank), low),
        ((rows, rank), high),
        ((feat_bits, feat_bits, rows, rank // feat_bits), low),
        ((feat_bits, feat_bits, rows, rank // feat_bits), low),
    ]
    turns = (feat_bits, half, blocks)
    counts = [
        (blocks,), (half, blocks), (blocks,), (half, blocks), (blocks,),
        turns, turns, turns, turns,
        (steps,), (half, steps), (half, steps), (half, steps), (steps,),
        (half, steps), (half, steps), (half, pieces), (pieces,), (pieces,), (),
        (feat_bits, feat_bits), (feat_bits, feat_bits),
    ]
    return arrays, counts


def kernel_fits(half, feat_bits, rows, weight_shape, rank):
    arrays, _ = kernel_scratch(half, feat_bits, rows, weight_shape, rank)
    size = sum(math.prod(shape) * jnp.dtype(kind).itemsize for shape, kind in arrays)
    return half > 1 and size <= VMEM_BYTES * 15 // 16


def hidden_of(tokens, gate_weight, up_weight, gate_scale, up_scale, partners, latent_in):
    half = lax.axis_size("tok") // PAIR // 2
    feat_bits = lax.axis_size("feat").bit_length() - 1
    rows, rank = tokens.shape[0], latent_in.shape[1]
    arrays, counts = kernel_scratch(half, feat_bits, rows, gate_weight.shape, rank)
    factor = latent_in.reshape(-1, math.gcd(gate_weight.shape[3], TILE), rank)
    scalars = pl.BlockSpec(memory_space=pltpu.SMEM)
    whole = pl.BlockSpec(memory_space=pl.ANY)
    return pl.pallas_call(
        functools.partial(hidden_kernel, half, feat_bits),
        out_shape=(
            jax.ShapeDtypeStruct(tokens.shape, jnp.bfloat16),
            jax.ShapeDtypeStruct((rows, rank), jnp.bfloat16),
        ),
        in_specs=[scalars] * 3 + [whole] * 4,
        out_specs=(whole, pl.BlockSpec(memory_space=pltpu.VMEM)),
        scratch_shapes=[pltpu.VMEM(*one) for one in arrays]
        + [pltpu.SemaphoreType.DMA(count) for count in counts],
        compiler_params=pltpu.CompilerParams(
            collective_id=0, has_side_effects=True, vmem_limit_bytes=VMEM_BYTES - 2**17
        ),
        name="hidden",
    )(partners, gate_scale, up_scale, tokens, gate_weight, up_weight, factor)


def fused(tokens, gate_weight, up_weight, gate_scale, up_scale, partners, latent_in, latent_out):
    hidden, latent = hidden_of(
        tokens, gate_weight, up_weight, gate_scale, up_scale, partners, latent_in
    )
    rank_term = jnp.dot(latent, latent_out, preferred_element_type=jnp.float32).astype(jnp.bfloat16)
    return hidden, rank_term


def solution(mesh):
    placed = (
        P("tok", "feat"),
        P("feat", None, "tok", None),
        P("feat", None, "tok", None),
        P("feat", None),
        P("feat", None),
        P(),
        P("feat", None),
        P(None, "feat"),
    )
    feat_bits = mesh.shape["feat"].bit_length() - 1
    half = mesh.shape["tok"] // PAIR // 2

    def sharded(function):
        return jax.shard_map(
            function,
            mesh=mesh,
            in_specs=placed,
            out_specs=(P("tok", "feat"), P("tok", "feat")),
            check_vma=False,
        )

    def run(*args):
        rows = args[0].shape[0] // mesh.shape["tok"]
        blocks, slot_count, depth, width = args[1].shape
        blocks //= mesh.shape["feat"]
        local = (blocks, slot_count, depth // mesh.shape["tok"], width)
        if kernel_fits(half, feat_bits, rows, local, args[6].shape[1]):
            return sharded(fused)(*args)
        return sharded(per_device)(*args)

    return run
```

```python
import functools
import math

import jax
import jax.numpy as jnp
from jax import lax
from jax.experimental import pallas as pl
from jax.experimental.pallas import tpu as pltpu
from jax.sharding import PartitionSpec as P


PAIR = 2


def swapped(value, axis, bit):
    mask = 2**bit
    pairs = [(source, source ^ mask) for source in range(lax.axis_size(axis))]
    return lax.ppermute(value, axis, pairs)


def moved(value, chip_pairs):
    pairs = [
        (PAIR * source + lane, PAIR * target + lane)
        for source, target in chip_pairs
        for lane in range(PAIR)
    ]
    return lax.ppermute(value, "tok", pairs)


def join_kernel(slots, gate, up, gate_scale, up_scale, joined, *, block):
    slot = slots[block, pl.program_id(0)]
    width = gate.shape[-1]
    for start, weight, scale in ((0, gate, gate_scale), (width, up, up_scale)):
        product = weight[0, 0].astype(jnp.float32) * scale[block, slot]
        joined[0, :, start : start + width] = product.astype(joined.dtype)


def joined_weights(slots, gate_weight, up_weight, gate_scale, up_scale, block):
    _, slot_count, rows, width = gate_weight.shape
    picked = pl.BlockSpec((1, 1, rows, width), lambda k, slots: (block, slots[block, k], 0, 0))
    whole = pl.BlockSpec(memory_space=pltpu.SMEM)
    size = slot_count * rows * width
    return pl.pallas_call(
        lambda *refs: join_kernel(*refs, block=block),
        out_shape=jax.ShapeDtypeStruct((slot_count, rows, 2 * width), jnp.bfloat16),
        grid_spec=pltpu.PrefetchScalarGridSpec(
            num_scalar_prefetch=1,
            grid=(slot_count,),
            in_specs=[picked, picked, whole, whole],
            out_specs=pl.BlockSpec((1, rows, 2 * width), lambda k, slots: (k, 0, 0)),
        ),
        cost_estimate=pl.CostEstimate(flops=2 * size, bytes_accessed=8 * size, transcendentals=0),
    )(slots, gate_weight, up_weight, gate_scale, up_scale)


def part_blocks(blocks):
    return max(1, blocks // 2)


def per_device(
    tokens, gate_weight, up_weight, gate_scale, up_scale, partners, latent_in, latent_out
):
    tok_rows = tokens.shape[0]
    blocks, slot_count, part_rows, blk_width = gate_weight.shape
    feat_count = lax.axis_size("feat")
    chips = lax.axis_size("tok") // PAIR
    half = chips // 2
    local_bits = blocks.bit_length() - 1
    feat_bits = feat_count.bit_length() - 1
    place = lax.axis_index("tok")
    chip, lane = place // PAIR, place % PAIR
    on_right = chip >= half
    distance = jnp.where(on_right, chip - half, half - 1 - chip)
    inward = [[(half - 1 - q, half - 1), (half + q, half)] for q in range(half)]
    across = [[(half - 1 - q, half), (half + q, half - 1)] for q in range(half)]
    outward = [[(half - 1, half - 1 - q), (half, half + q)] for q in range(half)]

    first_block = lax.axis_index("feat") * blocks
    block_ids = first_block + jnp.arange(blocks, dtype=jnp.int32)
    offsets = [0] + [1 << bit_pos for bit_pos in range(local_bits + feat_bits)]
    labels = jnp.bitwise_xor(block_ids[:, None], jnp.array(offsets, dtype=jnp.int32)[None, :])
    wanted = lax.dynamic_slice_in_dim(partners, first_block, blocks, 0)
    matched = wanted[:, :, None] == labels[:, None, :]
    slot_ids = jnp.arange(slot_count, dtype=jnp.int32)
    slots = jnp.sum(jnp.where(matched, slot_ids[None, :, None], 0), axis=1)
    ready = [
        joined_weights(slots, gate_weight, up_weight, gate_scale, up_scale, own_block)
        for own_block in range(blocks)
    ]

    pieces = tokens.T.reshape(blocks, chips, PAIR, part_rows, tok_rows).transpose(2, 1, 0, 3, 4)
    pieces = jnp.where(lane == 0, pieces, pieces[::-1])
    left, right = pieces[:, :half][:, ::-1], pieces[:, half:]
    near = jnp.where(on_right, right, left)
    far = jnp.where(on_right, left, right)
    step = part_blocks(blocks)
    far_parts = [far[:, :, start : start + step] for start in range(0, blocks, step)]
    from_far = [[moved(part, across[q]) for part in far_parts] for q in range(half)]
    from_near = [[near]] + [[moved(near, inward[q])] for q in range(1, half)]
    shipped = [
        [ready[block]]
        + [moved(ready[block], inward[q]) for q in range(1, half)]
        for block in range(blocks)
    ]

    def turned(groups):
        return [
            [[swapped(value, "feat", bit) for value in parts] for bit in range(feat_bits)]
            for parts in groups
        ]

    far_remote = turned(from_far)
    near_remote = turned(from_near)

    def block_of(parts, block):
        size = blocks // len(parts)
        return parts[block // size][:, :, block % size]

    def inputs_of(own_block, groups, remotes):
        rows = []
        for group, remote in zip(groups, remotes):
            picked = [block_of(group, own_block)]
            for bit_pos in range(local_bits):
                picked.append(block_of(group, own_block ^ 1 << bit_pos))
            for bit_pos in range(feat_bits):
                picked.append(block_of(remote[bit_pos], own_block))
            rows.append(jnp.stack(picked, axis=2).reshape(-1, tok_rows))
        return jnp.concatenate(rows, axis=1)

    def product(inputs, weights):
        return lax.dot_general(
            inputs, weights, (((0,), (0,)), ((), ())), preferred_element_type=jnp.float32
        )

    latent_part = jnp.zeros((tok_rows, latent_in.shape[1]), jnp.float32)
    hidden = []
    for own_block in range(blocks):
        mine = jnp.concatenate(shipped[own_block], axis=0)
        other = swapped(mine, "tok", 0)
        weights = jnp.concatenate([mine, other], axis=0).reshape(-1, 2 * blk_width)
        inputs = inputs_of(own_block, from_far, far_remote)
        away = product(inputs, weights).astype(jnp.bfloat16)
        back = moved(away, across[0])
        inputs = inputs_of(own_block, from_near, near_remote)
        home = product(inputs, weights)
        sums = home + back.astype(jnp.float32)
        done = (jax.nn.silu(sums[:, :blk_width]) * sums[:, blk_width:]).astype(jnp.bfloat16)
        block_hidden = done[:tok_rows]
        for q in range(1, half):
            share = done[q * tok_rows : (q + 1) * tok_rows]
            sent = moved(share, outward[q])
            block_hidden = jnp.where(distance == q, sent, block_hidden)
        hidden.append(block_hidden)
        rows = latent_in[own_block * blk_width : (own_block + 1) * blk_width]
        latent_part += jnp.dot(block_hidden, rows, preferred_element_type=jnp.float32)
    latent = latent_part
    for bit_pos in range(feat_bits):
        share = latent.astype(jnp.bfloat16)
        latent = share.astype(jnp.float32) + swapped(share, "feat", bit_pos).astype(jnp.float32)
    latent = latent.astype(jnp.bfloat16)
    rank_term = jnp.dot(latent, latent_out, preferred_element_type=jnp.float32).astype(jnp.bfloat16)
    return (jnp.concatenate(hidden, axis=1), rank_term)


MESH = pl.DeviceIdType.MESH
VMEM_BYTES = 64 * 2**20
TILE = 256
RING = 6
SPARE_BYTES = 3 * 2**20


def flipped(value, bit):
    mask = 2**bit
    return value + mask - 2 * mask * ((value // mask) % 2)


def hidden_kernel(
    half, feat_bits, partners, gate_scale, up_scale, tokens, gate, up, latent_in,
    hidden, latent, *scratch
):
    blocks, slot_count, part_rows, width = gate.shape
    rows = tokens.shape[0]
    parts = PAIR * half
    depth = parts * part_rows
    tile = math.gcd(width, TILE)
    cuts = width // tile
    steps = 2 * blocks * cuts
    pieces = blocks * cuts
    far_x, scratch = scratch[:half], scratch[half:]
    (
        weights, near_x, sent, got, ready, made, factor, total, share, shared, wanted,
        far_out, far_land, near_out, near_land, near_own,
        turn_far_out, turn_far_land, turn_near_out, turn_near_land,
        weight_out, weight_land, lane_out, lane_land, weight_own,
        sum_out, sum_land, give_out, give_land, keep_own, factor_own, share_out, share_land,
        wanted_own,
    ) = scratch
    ring = sent.shape[0]

    feat = lax.axis_index("feat")
    tok = lax.axis_index("tok")
    lane, chip = tok % PAIR, tok // PAIR
    side = chip // half
    distance = side * (chip - half) + (1 - side) * (half - 1 - chip)
    middle = (half - 1 + side) * PAIR + lane
    across = (half - side) * PAIR + lane
    partner = tok + 1 - 2 * lane

    def chip_of(which, q):
        return which * (half + q) + (1 - which) * (half - 1 - q)

    def tok_of(which, q):
        return chip_of(which, q) * PAIR + lane

    def part_of(q, which_lane):
        return (chip_of(side, q) - side * half) * PAIR + which_lane

    def remote(source, target, out, land, **where):
        return pltpu.make_async_remote_copy(
            src_ref=source,
            dst_ref=target,
            send_sem=out,
            recv_sem=land,
            device_id=where,
            device_id_type=MESH,
        )

    def columns(block, which):
        return pl.ds(pl.multiple_of(block * width + which * depth, math.gcd(width, depth)), depth)

    def far_copy(q, block, target):
        source = tokens.at[:, columns(block, 1 - side)]
        return remote(source, far_x[q].at[block], far_out, far_land.at[q, block], tok=target)

    def near_copy(q, block, target):
        source = tokens.at[:, columns(block, side)]
        return remote(source, near_x.at[block, q], near_out, near_land.at[q, block], tok=target)

    def far_turn(q, block, bit):
        source, place = [far_x[q].at[at] for at in (block, blocks * (1 + bit) + block)]
        semaphores = turn_far_out.at[q], turn_far_land.at[bit, q, block]
        return remote(source, place, *semaphores, feat=flipped(feat, bit))

    def near_turn(q, block, bit):
        source, place = [near_x.at[at, q] for at in (block, blocks * (1 + bit) + block)]
        semaphores = turn_near_out, turn_near_land.at[bit, q, block]
        return remote(source, place, *semaphores, feat=flipped(feat, bit))

    def settle(whole, semaphore):
        pltpu.make_async_copy(whole, whole, semaphore).wait()

    def stored(step):
        block, kind, cut = step // (2 * cuts), step // cuts % 2, step % cuts
        return (gate, up)[kind].at[block, :, :, pl.ds(cut * tile, tile)]

    def weight_copy(q, step, source, target):
        place = weights.at[step, :, part_of(q, lane)]
        return remote(source, place, weight_out, weight_land.at[q, step], tok=target)

    def lane_copy(q, step, source, which_lane):
        place = weights.at[step, :, part_of(q, which_lane)]
        source = place if source is None else source
        return remote(source, place, lane_out, lane_land.at[step], tok=partner)

    def own_copy(step, source):
        return pltpu.make_async_copy(
            source, weights.at[step, :, part_of(0, lane)], weight_own
        )

    def sum_copy(q, step):
        slot = step % ring
        return remote(sent.at[slot, q], got.at[step, q], sum_out.at[slot], sum_land.at[q, step], tok=across)

    def give_copy(q, piece, target):
        return remote(made.at[piece, q], made.at[piece, 0], give_out, give_land.at[piece], tok=target)

    def keep_copy(piece):
        place = hidden.at[:, pl.ds(pl.multiple_of(piece * tile, tile), tile)]
        return pltpu.make_async_copy(made.at[piece, 0], place, keep_own)

    def share_copy(stage, part):
        bit = (stage + part) % feat_bits
        semaphores = share_out, share_land.at[stage, part]
        return remote(share.at[stage, part], shared.at[stage, part], *semaphores, feat=flipped(feat, bit))

    factor_copy = pltpu.make_async_copy(latent_in, factor, factor_own)
    factor_copy.start()
    wanted_copy = pltpu.make_async_copy(partners, wanted, wanted_own)
    wanted_copy.start()
    barrier = pltpu.get_barrier_semaphore()

    def greet(peers):
        for peer in peers:
            pl.semaphore_signal(barrier, inc=1, device_id=peer, device_id_type=MESH)
        pl.semaphore_wait(barrier, len(peers))

    turns = [{"feat": flipped(feat, bit)} for bit in range(feat_bits)]

    def project(piece):
        total[...] += jnp.dot(
            made[piece, 0], factor[piece], preferred_element_type=jnp.float32
        )

    def clear():
        factor_copy.wait()
        wanted_copy.wait()
        total[...] = jnp.zeros_like(total)

    def near_after(block):
        return min(2 * cuts - 1 + 2 * block, steps - 1)

    early_steps = max(1, cuts - 1)
    first_home = max(near_after(blocks - 1) + 2, steps - 1 - (pieces - cuts))
    assert first_home < steps

    def outer(q):
        greet([{"tok": middle}, {"tok": across}] + turns)
        for step in range(early_steps):
            weight_copy(q, step, stored(step), middle).start()
        for block in range(blocks):
            far_copy(q, block, across).start()
        for step in range(early_steps, steps):
            weight_copy(q, step, stored(step), middle).start()
            for block in range(blocks):
                if near_after(block) == step:
                    near_copy(q, block, middle).start()
        clear()

        @pl.loop(0, pieces)
        def _(piece):
            give_copy(q, piece, middle).wait_recv()
            keep_copy(piece).start()
            project(piece)

        settle(far_x[0].at[pl.ds(0, blocks)], far_out)
        settle(near_x.at[pl.ds(0, blocks), 0], near_out)
        settle(weights.at[:, :, 0], weight_out)

    def inner():
        peers = [{"tok": partner}, {"tok": across}]
        for q in range(1, half):
            peers += [{"tok": tok_of(which, q)} for which in (side, 1 - side)]
        greet(peers + turns)
        for block in range(blocks):
            far_copy(0, block, across).start()
        for step in range(steps):
            lane_copy(0, step, stored(step), lane).start()
            own_copy(step, stored(step)).start()
        for block in range(blocks):
            source = tokens.at[:, columns(block, side)]
            pltpu.make_async_copy(source, near_x.at[block, 0], near_own).start()

        def take_far(q, block):
            far_copy(q, block, across).wait_recv()
            for bit in range(feat_bits):
                far_turn(q, block, bit).start()

        def turned_far(q):
            for block in range(blocks):
                for bit in range(feat_bits):
                    far_turn(q, block, bit).wait_recv()

        def source_of(block, slot):
            row = feat * blocks + block
            label = wanted[slot, row]
            place = label % blocks
            for bit in range(feat_bits):
                other = flipped(feat, bit) * blocks + block
                place = jnp.where(label == other, blocks * (1 + bit) + block, place)
            return place

        def sums(step, load):
            block, kind = step // (2 * cuts), step // cuts % 2
            value = None
            for slot in range(slot_count):
                scale = jnp.where(kind == 0, gate_scale[block, slot], up_scale[block, slot])
                inputs = load(source_of(block, slot))
                weight = weights[step, slot].reshape(depth, tile)
                term = jnp.dot(inputs, weight, preferred_element_type=jnp.float32) * scale
                value = term if value is None else value + term
            return value

        def near_sums(step):
            return sums(step, lambda at: near_x[at].reshape(half * rows, depth))

        def far_sums(step):
            return sums(step, lambda at: jnp.concatenate([x[at] for x in far_x], axis=0))

        def part_sums(q, step):
            return sums(step, lambda at: far_x[q][at])

        def pass_on(step):
            for q in range(1, half):
                weight_copy(q, step, stored(0), middle).wait_recv()
                lane_copy(q, step, None, lane).start()

        def pair_of(piece):
            step = piece // cuts * 2 * cuts + piece % cuts
            return step, step + cuts

        def gated(first, second):
            return (first / (1.0 + jnp.exp(-first)) * second).astype(made.dtype)

        def home(piece):
            for q in range(half):
                for step in pair_of(piece):
                    sum_copy(q, step).wait_recv()
            first, second = [
                near_sums(step) + got[step].reshape(half * rows, tile).astype(jnp.float32)
                for step in pair_of(piece)
            ]
            made[piece] = gated(first, second).reshape(half, rows, tile)
            for q in range(1, half):
                give_copy(q, piece, tok_of(side, q)).start()
            keep_copy(piece).start()
            project(piece)

        def early(q):
            @pl.loop(0, early_steps)
            def _(step):
                sent[step, q] = part_sums(q, step).astype(sent.dtype)
                sum_copy(q, step).start()

        for block in range(blocks):
            take_far(0, block)
        for step in range(early_steps):
            pass_on(step)
        clear()
        settle(weights.at[:, :, 0], weight_own)
        for q in range(1, half):
            take_far(q, 0)
        for step in range(early_steps):
            settle(weights.at[step, :, pl.ds(0, half)], lane_land.at[step])
        turned_far(0)
        early(0)
        for block in range(1, blocks):
            for q in range(1, half):
                take_far(q, block)
        settle(near_x.at[pl.ds(0, blocks), 0], near_own)
        for block in range(blocks):
            for bit in range(feat_bits):
                near_turn(0, block, bit).start()
        for q in range(1, half):
            turned_far(q)
            early(q)

        @pl.loop(early_steps, steps)
        def _(step):
            pass_on(step)
            settle(weights.at[step, :, pl.ds(0, half)], lane_land.at[step])

            @pl.when(step >= ring)
            def _():
                settle(sent.at[step % ring], sum_out.at[step % ring])

            sent[step % ring] = far_sums(step).astype(sent.dtype).reshape(half, rows, tile)
            for q in reversed(range(half)):
                sum_copy(q, step).start()
            for block in range(blocks):

                @pl.when(step == near_after(block))
                def _():
                    for q in range(1, half):
                        near_copy(q, block, middle).wait_recv()
                        for bit in range(feat_bits):
                            near_turn(q, block, bit).start()

            @pl.when(step == first_home)
            def _():
                for block in range(blocks):
                    for q in range(half):
                        for bit in range(feat_bits):
                            near_turn(q, block, bit).wait_recv()

            @pl.when((step >= first_home) & (step < first_home + pieces - cuts))
            def _():
                home(step - first_home)

        @pl.loop(steps, first_home + pieces - cuts)
        def _(step):
            home(step - first_home)

        @pl.loop(0, cuts)
        def _(cut):
            for kind, step in enumerate(pair_of(pieces - cuts + cut)):
                ready[kind, cut] = near_sums(step).reshape(half, rows, tile)

        @pl.loop(0, cuts)
        def _(cut):
            piece = pieces - cuts + cut
            for q in reversed(range(half)):
                values = []
                for kind, step in enumerate(pair_of(piece)):
                    sum_copy(q, step).wait_recv()
                    values.append(ready[kind, cut, q] + got[step, q].astype(jnp.float32))
                made[piece, q] = gated(*values)
                if q:
                    give_copy(q, piece, tok_of(side, q)).start()
            keep_copy(piece).start()
            project(piece)

    for q in range(1, half):
        pl.when(distance == q)(lambda q=q: outer(q))
    pl.when(distance == 0)(inner)

    part_width = total.shape[1] // feat_bits
    for stage in range(feat_bits):
        for part in range(feat_bits):
            span = pl.ds(part * part_width, part_width)
            share[stage, part] = total[:, span].astype(share.dtype)
            share_copy(stage, part).start()
        for part in range(feat_bits):
            span = pl.ds(part * part_width, part_width)
            share_copy(stage, part).wait_recv()
            ours = share[stage, part].astype(jnp.float32)
            total[:, span] = ours + shared[stage, part].astype(jnp.float32)
    latent[...] = total[...].astype(latent.dtype)

    settle(made.at[:, 0], keep_own)
    settle(share, share_out)

    @pl.when(distance == 0)
    def _():
        settle(far_x[0].at[pl.ds(0, blocks)], far_out)
        for q in range(half):
            settle(far_x[q].at[pl.ds(blocks, blocks * feat_bits)], turn_far_out.at[q])
        settle(near_x.at[pl.ds(blocks, blocks * feat_bits)], turn_near_out)
        settle(weights.at[:, :, pl.ds(0, half)], lane_out)
        for slot in range(ring):
            settle(sent.at[slot], sum_out.at[slot])
        settle(made.at[:, pl.ds(1, half - 1)], give_out)


def kernel_scratch(half, feat_bits, rows, weight_shape, rank):
    blocks, slot_count, part_rows, width = weight_shape
    tile = math.gcd(width, TILE)
    cuts = width // tile
    steps, pieces = 2 * blocks * cuts, blocks * cuts
    parts = PAIR * half
    sources = blocks * (1 + feat_bits)
    depth = parts * part_rows
    low, high = jnp.bfloat16, jnp.float32
    arrays = [((sources, rows, depth), low)] * half
    arrays += [
        ((steps, slot_count, parts, part_rows, tile), low),
        ((sources, half, rows, depth), low),
        ((min(RING, steps), half, rows, tile), low),
        ((steps, half, rows, tile), low),
        ((2, cuts, half, rows, tile), high),
        ((pieces, half, rows, tile), low),
        ((pieces, tile, rank), low),
        ((rows, rank), high),
        ((feat_bits, feat_bits, rows, rank // feat_bits), low),
        ((feat_bits, feat_bits, rows, rank // feat_bits), low),
    ]
    turns = (feat_bits, half, blocks)
    counts = [
        (), (half, blocks), (), (half, blocks), (),
        (half,), turns, (), turns,
        (), (half, steps), (), (steps,), (),
        (min(RING, steps),), (half, steps), (), (pieces,), (), (),
        (), (feat_bits, feat_bits), (),
    ]
    return arrays, counts


def kernel_bytes(arrays):
    return sum(math.prod(shape) * jnp.dtype(kind).itemsize for shape, kind in arrays)


def kernel_fits(half, feat_bits, rows, weight_shape, rank):
    arrays, _ = kernel_scratch(half, feat_bits, rows, weight_shape, rank)
    return half > 1 and kernel_bytes(arrays) <= VMEM_BYTES * 7 // 8


def hidden_of(tokens, gate_weight, up_weight, gate_scale, up_scale, partners, latent_in):
    half = lax.axis_size("tok") // PAIR // 2
    feat_bits = lax.axis_size("feat").bit_length() - 1
    rows, rank = tokens.shape[0], latent_in.shape[1]
    arrays, counts = kernel_scratch(half, feat_bits, rows, gate_weight.shape, rank)
    factor = latent_in.reshape(-1, math.gcd(gate_weight.shape[3], TILE), rank)
    scalars = pl.BlockSpec(memory_space=pltpu.SMEM)
    whole = pl.BlockSpec(memory_space=pl.ANY)
    return pl.pallas_call(
        functools.partial(hidden_kernel, half, feat_bits),
        out_shape=(
            jax.ShapeDtypeStruct(tokens.shape, jnp.bfloat16),
            jax.ShapeDtypeStruct((rows, rank), jnp.bfloat16),
        ),
        in_specs=[whole] + [scalars] * 2 + [whole] * 4,
        out_specs=(whole, pl.BlockSpec(memory_space=pltpu.VMEM)),
        scratch_shapes=[pltpu.VMEM(*one) for one in arrays]
        + [pltpu.SMEM(partners.shape[::-1], partners.dtype)]
        + [pltpu.SemaphoreType.DMA(count) for count in counts],
        compiler_params=pltpu.CompilerParams(
            collective_id=0, has_side_effects=True, vmem_limit_bytes=kernel_bytes(arrays) + SPARE_BYTES
        ),
        name="hidden",
    )(partners.T, gate_scale, up_scale, tokens, gate_weight, up_weight, factor)


def fused(tokens, gate_weight, up_weight, gate_scale, up_scale, partners, latent_in, latent_out):
    hidden, latent = hidden_of(
        tokens, gate_weight, up_weight, gate_scale, up_scale, partners, latent_in
    )
    rank_term = jnp.dot(latent, latent_out, preferred_element_type=jnp.float32).astype(jnp.bfloat16)
    return hidden, rank_term


def solution(mesh):
    placed = (
        P("tok", "feat"),
        P("feat", None, "tok", None),
        P("feat", None, "tok", None),
        P("feat", None),
        P("feat", None),
        P(),
        P("feat", None),
        P(None, "feat"),
    )
    feat_bits = mesh.shape["feat"].bit_length() - 1
    half = mesh.shape["tok"] // PAIR // 2

    def sharded(function):
        return jax.shard_map(
            function,
            mesh=mesh,
            in_specs=placed,
            out_specs=(P("tok", "feat"), P("tok", "feat")),
            check_vma=False,
        )

    def run(*args):
        rows = args[0].shape[0] // mesh.shape["tok"]
        blocks, slot_count, depth, width = args[1].shape
        blocks //= mesh.shape["feat"]
        local = (blocks, slot_count, depth // mesh.shape["tok"], width)
        if kernel_fits(half, feat_bits, rows, local, args[6].shape[1]):
            return sharded(fused)(*args)
        return sharded(per_device)(*args)

    return run
```

```python
import functools
import math

import jax
import jax.numpy as jnp
from jax import lax
from jax.experimental import pallas as pl
from jax.experimental.pallas import tpu as pltpu
from jax.sharding import PartitionSpec as P


PAIR = 2


def swapped(value, axis, bit):
    mask = 2**bit
    pairs = [(source, source ^ mask) for source in range(lax.axis_size(axis))]
    return lax.ppermute(value, axis, pairs)


def moved(value, chip_pairs):
    pairs = [
        (PAIR * source + lane, PAIR * target + lane)
        for source, target in chip_pairs
        for lane in range(PAIR)
    ]
    return lax.ppermute(value, "tok", pairs)


def join_kernel(slots, gate, up, gate_scale, up_scale, joined, *, block):
    slot = slots[block, pl.program_id(0)]
    width = gate.shape[-1]
    for start, weight, scale in ((0, gate, gate_scale), (width, up, up_scale)):
        product = weight[0, 0].astype(jnp.float32) * scale[block, slot]
        joined[0, :, start : start + width] = product.astype(joined.dtype)


def joined_weights(slots, gate_weight, up_weight, gate_scale, up_scale, block):
    _, slot_count, rows, width = gate_weight.shape
    picked = pl.BlockSpec((1, 1, rows, width), lambda k, slots: (block, slots[block, k], 0, 0))
    whole = pl.BlockSpec(memory_space=pltpu.SMEM)
    size = slot_count * rows * width
    return pl.pallas_call(
        lambda *refs: join_kernel(*refs, block=block),
        out_shape=jax.ShapeDtypeStruct((slot_count, rows, 2 * width), jnp.bfloat16),
        grid_spec=pltpu.PrefetchScalarGridSpec(
            num_scalar_prefetch=1,
            grid=(slot_count,),
            in_specs=[picked, picked, whole, whole],
            out_specs=pl.BlockSpec((1, rows, 2 * width), lambda k, slots: (k, 0, 0)),
        ),
        cost_estimate=pl.CostEstimate(flops=2 * size, bytes_accessed=8 * size, transcendentals=0),
    )(slots, gate_weight, up_weight, gate_scale, up_scale)


def part_blocks(blocks):
    return max(1, blocks // 2)


def per_device(
    tokens, gate_weight, up_weight, gate_scale, up_scale, partners, latent_in, latent_out
):
    tok_rows = tokens.shape[0]
    blocks, slot_count, part_rows, blk_width = gate_weight.shape
    feat_count = lax.axis_size("feat")
    chips = lax.axis_size("tok") // PAIR
    half = chips // 2
    local_bits = blocks.bit_length() - 1
    feat_bits = feat_count.bit_length() - 1
    place = lax.axis_index("tok")
    chip, lane = place // PAIR, place % PAIR
    on_right = chip >= half
    distance = jnp.where(on_right, chip - half, half - 1 - chip)
    inward = [[(half - 1 - q, half - 1), (half + q, half)] for q in range(half)]
    across = [[(half - 1 - q, half), (half + q, half - 1)] for q in range(half)]
    outward = [[(half - 1, half - 1 - q), (half, half + q)] for q in range(half)]

    first_block = lax.axis_index("feat") * blocks
    block_ids = first_block + jnp.arange(blocks, dtype=jnp.int32)
    offsets = [0] + [1 << bit_pos for bit_pos in range(local_bits + feat_bits)]
    labels = jnp.bitwise_xor(block_ids[:, None], jnp.array(offsets, dtype=jnp.int32)[None, :])
    wanted = lax.dynamic_slice_in_dim(partners, first_block, blocks, 0)
    matched = wanted[:, :, None] == labels[:, None, :]
    slot_ids = jnp.arange(slot_count, dtype=jnp.int32)
    slots = jnp.sum(jnp.where(matched, slot_ids[None, :, None], 0), axis=1)
    ready = [
        joined_weights(slots, gate_weight, up_weight, gate_scale, up_scale, own_block)
        for own_block in range(blocks)
    ]

    pieces = tokens.T.reshape(blocks, chips, PAIR, part_rows, tok_rows).transpose(2, 1, 0, 3, 4)
    pieces = jnp.where(lane == 0, pieces, pieces[::-1])
    left, right = pieces[:, :half][:, ::-1], pieces[:, half:]
    near = jnp.where(on_right, right, left)
    far = jnp.where(on_right, left, right)
    step = part_blocks(blocks)
    far_parts = [far[:, :, start : start + step] for start in range(0, blocks, step)]
    from_far = [[moved(part, across[q]) for part in far_parts] for q in range(half)]
    from_near = [[near]] + [[moved(near, inward[q])] for q in range(1, half)]
    shipped = [
        [ready[block]]
        + [moved(ready[block], inward[q]) for q in range(1, half)]
        for block in range(blocks)
    ]

    def turned(groups):
        return [
            [[swapped(value, "feat", bit) for value in parts] for bit in range(feat_bits)]
            for parts in groups
        ]

    far_remote = turned(from_far)
    near_remote = turned(from_near)

    def block_of(parts, block):
        size = blocks // len(parts)
        return parts[block // size][:, :, block % size]

    def inputs_of(own_block, groups, remotes):
        rows = []
        for group, remote in zip(groups, remotes):
            picked = [block_of(group, own_block)]
            for bit_pos in range(local_bits):
                picked.append(block_of(group, own_block ^ 1 << bit_pos))
            for bit_pos in range(feat_bits):
                picked.append(block_of(remote[bit_pos], own_block))
            rows.append(jnp.stack(picked, axis=2).reshape(-1, tok_rows))
        return jnp.concatenate(rows, axis=1)

    def product(inputs, weights):
        return lax.dot_general(
            inputs, weights, (((0,), (0,)), ((), ())), preferred_element_type=jnp.float32
        )

    latent_part = jnp.zeros((tok_rows, latent_in.shape[1]), jnp.float32)
    hidden = []
    for own_block in range(blocks):
        mine = jnp.concatenate(shipped[own_block], axis=0)
        other = swapped(mine, "tok", 0)
        weights = jnp.concatenate([mine, other], axis=0).reshape(-1, 2 * blk_width)
        inputs = inputs_of(own_block, from_far, far_remote)
        away = product(inputs, weights).astype(jnp.bfloat16)
        back = moved(away, across[0])
        inputs = inputs_of(own_block, from_near, near_remote)
        home = product(inputs, weights)
        sums = home + back.astype(jnp.float32)
        done = (jax.nn.silu(sums[:, :blk_width]) * sums[:, blk_width:]).astype(jnp.bfloat16)
        block_hidden = done[:tok_rows]
        for q in range(1, half):
            share = done[q * tok_rows : (q + 1) * tok_rows]
            sent = moved(share, outward[q])
            block_hidden = jnp.where(distance == q, sent, block_hidden)
        hidden.append(block_hidden)
        rows = latent_in[own_block * blk_width : (own_block + 1) * blk_width]
        latent_part += jnp.dot(block_hidden, rows, preferred_element_type=jnp.float32)
    latent = latent_part
    for bit_pos in range(feat_bits):
        share = latent.astype(jnp.bfloat16)
        latent = share.astype(jnp.float32) + swapped(share, "feat", bit_pos).astype(jnp.float32)
    latent = latent.astype(jnp.bfloat16)
    rank_term = jnp.dot(latent, latent_out, preferred_element_type=jnp.float32).astype(jnp.bfloat16)
    return (jnp.concatenate(hidden, axis=1), rank_term)


MESH = pl.DeviceIdType.MESH
VMEM_BYTES = 64 * 2**20
TILE = 256
RING = 6
GROUPS = 2
OWN = 8
SPARE_BYTES = 3 * 2**20


def flipped(value, bit):
    mask = 2**bit
    return value + mask - 2 * mask * ((value // mask) % 2)


def hidden_kernel(
    half, feat_bits, partners, gate_scale, up_scale, tokens, gate, up, latent_in,
    hidden, latent, *scratch
):
    blocks, slot_count, part_rows, width = gate.shape
    rows = tokens.shape[0]
    parts = PAIR * half
    depth = parts * part_rows
    tile = math.gcd(width, TILE)
    cuts = width // tile
    steps = 2 * blocks * cuts
    pieces = blocks * cuts
    far_x, scratch = scratch[:half], scratch[half:]
    (
        passing, weights, near_x, sent, got, ready, made, factor, total, share, shared, wanted,
        far_out, far_land, pass_land, pass_out, near_out, near_land, near_own,
        turn_far_out, turn_far_land, turn_near_out, turn_near_land,
        weight_out, weight_land, lane_out, lane_land, weight_own,
        sum_out, sum_land, give_out, give_land, keep_own, factor_own, share_out, share_land,
        wanted_own,
    ) = scratch
    ring = sent.shape[0]
    part_width = total.shape[1] // feat_bits
    group_rows = rows // GROUPS

    feat = lax.axis_index("feat")
    tok = lax.axis_index("tok")
    lane, chip = tok % PAIR, tok // PAIR
    side = chip // half
    distance = side * (chip - half) + (1 - side) * (half - 1 - chip)
    middle = (half - 1 + side) * PAIR + lane
    across = (half - side) * PAIR + lane
    partner = tok + 1 - 2 * lane

    def chip_of(which, q):
        return which * (half + q) + (1 - which) * (half - 1 - q)

    def tok_of(which, q):
        return chip_of(which, q) * PAIR + lane

    def part_of(q, which_lane):
        return (chip_of(side, q) - side * half) * PAIR + which_lane

    def remote(source, target, out, land, **where):
        return pltpu.make_async_remote_copy(
            src_ref=source,
            dst_ref=target,
            send_sem=out,
            recv_sem=land,
            device_id=where,
            device_id_type=MESH,
        )

    def columns(block, which):
        return pl.ds(pl.multiple_of(block * width + which * depth, math.gcd(width, depth)), depth)

    def far_copy(q, block, target):
        source = tokens.at[:, columns(block, 1 - side)]
        return remote(source, far_x[q].at[block], far_out, far_land.at[q, block], tok=target)

    def pass_copy(q, block, target):
        source = tokens.at[:, columns(block, 1 - side)]
        place = passing.at[q - 1, block]
        return remote(source, place, far_out, pass_land.at[q - 1, block], tok=target)

    def relay_copy(q, block):
        source, place = passing.at[q - 1, block], far_x[q].at[block]
        return remote(source, place, pass_out, far_land.at[q, block], tok=across)

    def near_copy(q, block, target):
        source = tokens.at[:, columns(block, side)]
        return remote(source, near_x.at[block, q], near_out, near_land.at[q, block], tok=target)

    def far_turn(q, block, bit):
        source, place = [far_x[q].at[at] for at in (block, blocks * (1 + bit) + block)]
        semaphores = turn_far_out.at[q], turn_far_land.at[bit, q, block]
        return remote(source, place, *semaphores, feat=flipped(feat, bit))

    def near_turn(q, block, bit):
        source, place = [near_x.at[at, q] for at in (block, blocks * (1 + bit) + block)]
        semaphores = turn_near_out, turn_near_land.at[bit, q, block]
        return remote(source, place, *semaphores, feat=flipped(feat, bit))

    def settle(whole, semaphore):
        pltpu.make_async_copy(whole, whole, semaphore).wait()

    def stored(step):
        block, kind, cut = step // (2 * cuts), step // cuts % 2, step % cuts
        return (gate, up)[kind].at[block, :, :, pl.ds(cut * tile, tile)]

    def weight_copy(q, step, source, target):
        place = weights.at[step, :, part_of(q, lane)]
        return remote(source, place, weight_out, weight_land.at[q - 1, step], tok=target)

    def lane_copy(q, step):
        place = weights.at[step, :, part_of(q, lane)]
        return remote(place, place, lane_out, lane_land.at[step], tok=partner)

    def own_copy(step, source):
        place = weights.at[step, :, part_of(0, lane)]
        return pltpu.make_async_copy(source, place, weight_own.at[step % weight_own.shape[0]])

    def load(step):
        for kind in range(2):

            @pl.when(step // cuts % 2 == kind)
            def _():
                place = pl.ds(pl.multiple_of(step % cuts * tile, tile), tile)
                own_copy(step, (gate, up)[kind].at[step // (2 * cuts), :, :, place]).start()

    def hand(step):
        own_copy(step, stored(0)).wait()
        lane_copy(0, step).start()

    def sum_copy(q, step):
        slot = step % ring
        return remote(sent.at[slot, q], got.at[step, q], sum_out.at[slot], sum_land.at[q, step], tok=across)

    def give_copy(q, piece, target):
        return remote(made.at[piece, q], made.at[piece, 0], give_out, give_land.at[piece], tok=target)

    def keep_copy(piece):
        place = hidden.at[:, pl.ds(pl.multiple_of(piece * tile, tile), tile)]
        return pltpu.make_async_copy(made.at[piece, 0], place, keep_own)

    def share_copy(stage, part, group):
        bit = (stage + part) % feat_bits
        at = (stage, part, pl.ds(group * group_rows, group_rows))
        semaphores = share_out, share_land.at[stage, part, group]
        return remote(share.at[at], shared.at[at], *semaphores, feat=flipped(feat, bit))

    factor_copy = pltpu.make_async_copy(latent_in, factor, factor_own)
    wanted_copy = pltpu.make_async_copy(partners, wanted, wanted_own)
    wanted_copy.start()
    barrier = pltpu.get_barrier_semaphore()

    def greet(peers):
        for peer in peers:
            pl.semaphore_signal(barrier, inc=1, device_id=peer, device_id_type=MESH)
        pl.semaphore_wait(barrier, len(peers))

    turns = [{"feat": flipped(feat, bit)} for bit in range(feat_bits)]

    def project(piece):
        total[...] += jnp.dot(
            made[piece, 0], factor[piece], preferred_element_type=jnp.float32
        )

    def clear():
        factor_copy.start()
        total[...] = jnp.zeros_like(total)

    def near_after(block):
        return min(2 * cuts - 1 + 2 * block, steps - 1)

    early_steps = cuts
    ahead = min(3, (steps - early_steps) // 2)
    held = steps - 2 if cuts > 1 else steps
    first_home = max(near_after(blocks - 1) + 2, steps - cuts + 1 - (pieces - cuts))
    assert first_home < steps

    def outer(q):
        greet([{"tok": middle}] + turns)
        for block in range(blocks):
            pass_copy(q, block, middle).start()
        for step in range(steps):
            weight_copy(q, step, stored(step), middle).start()
            for block in range(blocks):
                if near_after(block) == step:
                    near_copy(q, block, middle).start()
        clear()
        wanted_copy.wait()
        factor_copy.wait()

        @pl.loop(0, pieces)
        def _(piece):
            give_copy(q, piece, middle).wait_recv()
            keep_copy(piece).start()
            project(piece)

        settle(far_x[0].at[pl.ds(0, blocks)], far_out)
        settle(near_x.at[pl.ds(0, blocks), 0], near_out)
        settle(weights.at[:, :, 0], weight_out)

    def inner():
        peers = [{"tok": partner}, {"tok": across}]
        for q in range(1, half):
            peers.append({"tok": tok_of(side, q)})
        greet(peers + turns)
        for block in range(blocks):
            far_copy(0, block, across).start()
        for step in range(early_steps):
            own_copy(step, stored(step)).start()

        def take_far(q, block):
            far_copy(q, block, across).wait_recv()
            for bit in range(feat_bits):
                far_turn(q, block, bit).start()

        def turned_far(q):
            for block in range(blocks):
                for bit in range(feat_bits):
                    far_turn(q, block, bit).wait_recv()

        def source_of(block, slot):
            row = feat * blocks + block
            label = wanted[slot, row]
            place = label % blocks
            for bit in range(feat_bits):
                other = flipped(feat, bit) * blocks + block
                place = jnp.where(label == other, blocks * (1 + bit) + block, place)
            return place

        def sums(step, load):
            block, kind = step // (2 * cuts), step // cuts % 2
            value = None
            for slot in range(slot_count):
                scale = jnp.where(kind == 0, gate_scale[block, slot], up_scale[block, slot])
                inputs = load(source_of(block, slot))
                weight = weights[step, slot].reshape(depth, tile)
                term = jnp.dot(inputs, weight, preferred_element_type=jnp.float32) * scale
                value = term if value is None else value + term
            return value

        def near_sums(step):
            return sums(step, lambda at: near_x[at].reshape(half * rows, depth))

        def far_sums(step):
            return sums(step, lambda at: jnp.concatenate([x[at] for x in far_x], axis=0))

        def part_sums(q, step):
            return sums(step, lambda at: far_x[q][at])

        def pass_on(step):
            for q in range(1, half):
                weight_copy(q, step, stored(0), middle).wait_recv()
                lane_copy(q, step).start()

        def pair_of(piece):
            step = piece // cuts * 2 * cuts + piece % cuts
            return step, step + cuts

        def gated(first, second):
            return (first / (1.0 + jnp.exp(-first)) * second).astype(made.dtype)

        def home(piece):
            for q in range(half):
                for step in pair_of(piece):
                    sum_copy(q, step).wait_recv()
            first, second = [
                near_sums(step) + got[step].reshape(half * rows, tile).astype(jnp.float32)
                for step in pair_of(piece)
            ]
            made[piece] = gated(first, second).reshape(half, rows, tile)
            for q in range(1, half):
                give_copy(q, piece, tok_of(side, q)).start()
            keep_copy(piece).start()
            project(piece)

        def early(q, step):
            sent[step, q] = part_sums(q, step).astype(sent.dtype)
            sum_copy(q, step).start()

        for block in range(blocks):
            take_far(0, block)
            for q in range(1, half):
                pass_copy(q, block, middle).wait_recv()
                relay_copy(q, block).start()
        wanted_copy.wait()
        for step in range(early_steps):
            hand(step)
        coming = list(range(blocks))

        def next_far():
            if coming:
                block = coming.pop(0)
                for q in range(1, half):
                    take_far(q, block)

        next_far()
        for step in range(early_steps):
            pass_on(step)
            if step == 0:
                next_far()
                turned_far(0)
            settle(weights.at[step, :, pl.ds(0, half)], lane_land.at[step])
            early(0, step)
            next_far()
        while coming:
            next_far()
        for step in range(early_steps, early_steps + ahead):
            own_copy(step, stored(step)).start()
        for block in range(blocks):
            source = tokens.at[:, columns(block, side)]
            pltpu.make_async_copy(source, near_x.at[block, 0], near_own).start()
        for step in range(early_steps, early_steps + ahead):
            hand(step)
        for step in range(early_steps + ahead, early_steps + 2 * ahead):
            own_copy(step, stored(step)).start()
        settle(near_x.at[pl.ds(0, blocks), 0], near_own)
        for block in range(blocks):
            for bit in range(feat_bits):
                near_turn(0, block, bit).start()
        for q in range(1, half):
            turned_far(q)

            @pl.loop(0, early_steps)
            def _(step):
                early(q, step)

        clear()

        @pl.loop(early_steps, steps)
        def _(step):
            pass_on(step)

            @pl.when(step + ahead < steps)
            def _():
                hand(step + ahead)

            @pl.when(step + 2 * ahead < steps)
            def _():
                load(step + 2 * ahead)

            settle(weights.at[step, :, pl.ds(0, half)], lane_land.at[step])

            @pl.when(step >= ring)
            def _():
                settle(sent.at[step % ring], sum_out.at[step % ring])

            sent[step % ring] = far_sums(step).astype(sent.dtype).reshape(half, rows, tile)
            for q in reversed(range(1, half)):
                sum_copy(q, step).start()

            @pl.when(step < held)
            def _():
                sum_copy(0, step).start()

            @pl.when(step == steps - 1)
            def _():
                for other in range(held, steps):
                    sum_copy(0, other).start()

            for block in range(blocks):

                @pl.when(step == near_after(block))
                def _():
                    for q in range(1, half):
                        near_copy(q, block, middle).wait_recv()
                        for bit in range(feat_bits):
                            near_turn(q, block, bit).start()

            @pl.when(step == first_home)
            def _():
                for block in range(blocks):
                    for q in range(half):
                        for bit in range(feat_bits):
                            near_turn(q, block, bit).wait_recv()
                factor_copy.wait()

            @pl.when((step >= first_home) & (step < first_home + pieces - cuts))
            def _():
                home(step - first_home)

            @pl.when(step >= steps - cuts)
            def _():
                cut = step - (steps - cuts)
                for kind, other in enumerate(pair_of(pieces - cuts + cut)):
                    ready[kind, cut] = near_sums(other).reshape(half, rows, tile)

        @pl.loop(steps, first_home + pieces - cuts)
        def _(step):
            home(step - first_home)

        def last(q, cut):
            piece = pieces - cuts + cut
            values = []
            for kind, step in enumerate(pair_of(piece)):
                sum_copy(q, step).wait_recv()
                values.append(ready[kind, cut, q] + got[step, q].astype(jnp.float32))
            made[piece, q] = gated(*values)
            if q:
                give_copy(q, piece, tok_of(side, q)).start()
            else:
                keep_copy(piece).start()
                project(piece)

        split = cuts - (steps - held)
        for cut_range in (range(split), range(split, cuts)):
            for q in reversed(range(half)):
                for cut in cut_range:
                    last(q, cut)

    for q in range(1, half):
        pl.when(distance == q)(lambda q=q: outer(q))
    pl.when(distance == 0)(inner)

    def span(part):
        return pl.ds(part * part_width, part_width)

    for stage in range(feat_bits + 1):
        for group in range(GROUPS):
            lines = pl.ds(group * group_rows, group_rows)
            for part in range(feat_bits):
                if stage:
                    share_copy(stage - 1, part, group).wait_recv()
                    ours = share[stage - 1, part, lines].astype(jnp.float32)
                    value = ours + shared[stage - 1, part, lines].astype(jnp.float32)
                else:
                    value = total[lines, span(part)]
                if stage < feat_bits:
                    share[stage, part, lines] = value.astype(share.dtype)
                    share_copy(stage, part, group).start()
                else:
                    latent[lines, span(part)] = value.astype(latent.dtype)

    settle(made.at[:, 0], keep_own)
    settle(share, share_out)

    @pl.when(distance == 0)
    def _():
        settle(far_x[0].at[pl.ds(0, blocks)], far_out)
        settle(passing, pass_out)
        for q in range(half):
            settle(far_x[q].at[pl.ds(blocks, blocks * feat_bits)], turn_far_out.at[q])
        settle(near_x.at[pl.ds(blocks, blocks * feat_bits)], turn_near_out)
        settle(weights.at[:, :, pl.ds(0, half)], lane_out)
        for slot in range(ring):
            settle(sent.at[slot], sum_out.at[slot])
        settle(made.at[:, pl.ds(1, half - 1)], give_out)


def kernel_scratch(half, feat_bits, rows, weight_shape, rank):
    blocks, slot_count, part_rows, width = weight_shape
    tile = math.gcd(width, TILE)
    cuts = width // tile
    steps, pieces = 2 * blocks * cuts, blocks * cuts
    parts = PAIR * half
    sources = blocks * (1 + feat_bits)
    depth = parts * part_rows
    low, high = jnp.bfloat16, jnp.float32
    arrays = [((sources, rows, depth), low)] * half
    arrays += [
        ((half - 1, blocks, rows, depth), low),
        ((steps, slot_count, parts, part_rows, tile), low),
        ((sources, half, rows, depth), low),
        ((min(RING, steps), half, rows, tile), low),
        ((steps, half, rows, tile), low),
        ((2, cuts, half, rows, tile), high),
        ((pieces, half, rows, tile), low),
        ((pieces, tile, rank), low),
        ((rows, rank), high),
        ((feat_bits, feat_bits, rows, rank // feat_bits), low),
        ((feat_bits, feat_bits, rows, rank // feat_bits), low),
    ]
    turns = (feat_bits, half, blocks)
    counts = [
        (), (half, blocks), (half - 1, blocks), (), (), (half, blocks), (),
        (half,), turns, (), turns,
        (), (half - 1, steps), (), (steps,), (min(OWN, steps),),
        (min(RING, steps),), (half, steps), (), (pieces,), (), (),
        (), (feat_bits, feat_bits, GROUPS), (),
    ]
    return arrays, counts


def kernel_bytes(arrays):
    return sum(math.prod(shape) * jnp.dtype(kind).itemsize for shape, kind in arrays)


def kernel_fits(half, feat_bits, rows, weight_shape, rank):
    arrays, _ = kernel_scratch(half, feat_bits, rows, weight_shape, rank)
    return half > 1 and kernel_bytes(arrays) <= VMEM_BYTES * 7 // 8


def hidden_of(tokens, gate_weight, up_weight, gate_scale, up_scale, partners, latent_in):
    half = lax.axis_size("tok") // PAIR // 2
    feat_bits = lax.axis_size("feat").bit_length() - 1
    rows, rank = tokens.shape[0], latent_in.shape[1]
    arrays, counts = kernel_scratch(half, feat_bits, rows, gate_weight.shape, rank)
    factor = latent_in.reshape(-1, math.gcd(gate_weight.shape[3], TILE), rank)
    scalars = pl.BlockSpec(memory_space=pltpu.SMEM)
    whole = pl.BlockSpec(memory_space=pl.ANY)
    return pl.pallas_call(
        functools.partial(hidden_kernel, half, feat_bits),
        out_shape=(
            jax.ShapeDtypeStruct(tokens.shape, jnp.bfloat16),
            pltpu.VMEM((rows, rank), jnp.bfloat16),
        ),
        in_specs=[whole] + [scalars] * 2 + [whole] * 4,
        out_specs=(whole, pl.BlockSpec(memory_space=pltpu.VMEM)),
        scratch_shapes=[pltpu.VMEM(*one) for one in arrays]
        + [pltpu.SMEM(partners.shape[::-1], partners.dtype)]
        + [pltpu.SemaphoreType.DMA(count) for count in counts],
        compiler_params=pltpu.CompilerParams(
            collective_id=0, has_side_effects=True, vmem_limit_bytes=kernel_bytes(arrays) + SPARE_BYTES
        ),
        name="hidden",
    )(partners.T, gate_scale, up_scale, tokens, gate_weight, up_weight, factor)


def rank_kernel(latent, factor, given, rank_term, hidden, made, held, taken, kept, written):
    width = made.shape[1]
    tile = math.gcd(width, 3 * TILE)
    take = pltpu.make_async_copy(given, held, taken)
    take.start()
    keep = pltpu.make_async_copy(held, hidden, kept)
    for at in range(width // tile):
        span = pl.ds(at * tile, tile)
        value = jnp.dot(latent[...], factor[:, span], preferred_element_type=jnp.float32)
        made[:, span] = value.astype(made.dtype)
        pltpu.make_async_copy(made.at[:, span], rank_term.at[:, span], written).start()
        if at == 0:
            take.wait()
            keep.start()
    keep.wait()
    pltpu.make_async_copy(made, rank_term, written).wait()


def rank_of(latent, latent_out, hidden):
    inside = pl.BlockSpec(memory_space=pltpu.VMEM)
    whole = pl.BlockSpec(memory_space=pl.ANY)
    shape = jax.ShapeDtypeStruct(hidden.shape, hidden.dtype)
    return pl.pallas_call(
        rank_kernel,
        out_shape=(shape, shape),
        in_specs=[inside, inside, pl.BlockSpec(memory_space=pltpu.HBM)],
        out_specs=(whole, whole),
        scratch_shapes=[pltpu.VMEM(hidden.shape, hidden.dtype)] * 2
        + [pltpu.SemaphoreType.DMA(())] * 3,
        compiler_params=pltpu.CompilerParams(vmem_limit_bytes=6 * hidden.size),
        cost_estimate=pl.CostEstimate(
            flops=2 * latent.size * latent_out.shape[1],
            bytes_accessed=6 * hidden.size,
            transcendentals=0,
        ),
        name="rank",
    )(latent, pltpu.with_memory_space_constraint(latent_out, pltpu.VMEM), pltpu.with_memory_space_constraint(hidden, pltpu.HBM))


def fused(tokens, gate_weight, up_weight, gate_scale, up_scale, partners, latent_in, latent_out):
    hidden, latent = hidden_of(
        tokens, gate_weight, up_weight, gate_scale, up_scale, partners, latent_in
    )
    rank_term, hidden = rank_of(latent, latent_out, hidden)
    return hidden, rank_term


def solution(mesh):
    placed = (
        P("tok", "feat"),
        P("feat", None, "tok", None),
        P("feat", None, "tok", None),
        P("feat", None),
        P("feat", None),
        P(),
        P("feat", None),
        P(None, "feat"),
    )
    feat_bits = mesh.shape["feat"].bit_length() - 1
    half = mesh.shape["tok"] // PAIR // 2

    def sharded(function):
        return jax.shard_map(
            function,
            mesh=mesh,
            in_specs=placed,
            out_specs=(P("tok", "feat"), P("tok", "feat")),
            check_vma=False,
        )

    def run(*args):
        rows = args[0].shape[0] // mesh.shape["tok"]
        blocks, slot_count, depth, width = args[1].shape
        blocks //= mesh.shape["feat"]
        local = (blocks, slot_count, depth // mesh.shape["tok"], width)
        if kernel_fits(half, feat_bits, rows, local, args[6].shape[1]):
            return sharded(fused)(*args)
        return sharded(per_device)(*args)

    return run
```
